32 devices in a mesh: expert: 4 (over y, core), dp: 8 (over z, x).
Axes of the slice: x: 2, y: 2, z: 4, core: 2. Of those that a mesh axis runs over, the one named last changes fastest.
Arguments:
- tokens: bfloat16 [512, 4096], P(('expert', 'dp')), may hold values from -6 to 6
- routes: int32 [512, 2], P(('expert', 'dp')), may hold values from 0 to 3, all different within a row; in each aligned block of 16 rows (0 to 15, 16 to 31, ...) at most 12 rows name the same one
- router_logits: float32 [512, 2], P(('expert', 'dp')), may hold values from -0.6 to 0.6
- gate_weight: bfloat16 [4, 4096, 12288], P('expert', None, 'dp'), may hold values from -0.09375 to 0.09375
- up_weight: bfloat16 [4, 4096, 12288], P('expert', None, 'dp'), may hold values from -0.09375 to 0.09375
- down_weight: bfloat16 [4, 12288, 4096], P('expert', 'dp'), may hold values from -0.0546875 to 0.0546875
Outputs:
- mixed_out: bfloat16 [512, 4096], P(('expert', 'dp'))
The draws below stay inside these ranges and needn't reach their ends.
Inputs may be any that keep to these rules, and one draw needn't show every extreme that they name: `routes`: each token names 2 different experts; among the tokens of one device no expert is named more than 12 times, a bound that some block reaches.
All inputs are finite; a program needn't handle non-finite values.
Results may differ from the reference program's by a relative error of at most 0.014.
Values may be sent and summed in bfloat16 or wider, within the bound.
A program may use at most 128 MiB of HBM per device.

```python
import math
import jax
import jax.numpy as jnp
import numpy as np
from jax import lax

D = 4096
FF = 12288
TOPK = 2
TOK_DEV = 16
EXPERTS = 4
TOKENS = 512
C = 12
FFS = 1536
N_EXPERT = 4
N_DP = 8


def level_of(stream_key, dims, cuts, smallest, high):
    def one(axis_at, blocks):
        steps = jax.random.uniform(jax.random.fold_in(jax.random.fold_in(stream_key, 6), axis_at), (blocks,), jnp.float32, smallest / len(cuts), high / len(cuts))
        return jnp.repeat(jnp.exp(steps), dims[axis_at] // blocks).reshape((-1,) + (1,) * (len(dims) - axis_at - 1))

    loudness = one(*cuts[0])
    for cut in cuts[1:]:
        loudness = loudness * one(*cut)
    return loudness


def assign_block(own_key, own, number, rows, count, top, bound, slope):
    sequence = jax.random.permutation(own_key, count)
    crowded, ordinary = portions_of(count, rows * top, bound, slope, True), portions_of(count, rows * top, bound, slope, False)
    places = jnp.arange(count)

    def named(sizes, turn):
        used = int((sizes > 0).sum())
        fixed = max(1, used // 4)
        moved = fixed + (places - fixed + turn * (used - fixed)) % max(1, count - fixed)
        return jnp.zeros((count,), jnp.int32).at[sequence[jnp.where(places < fixed, places, moved)]].set(jnp.asarray(sizes, jnp.int32))

    sizes = jnp.where(number % 4 == 0, named(crowded, number // 4), named(ordinary, number - number // 4 - 1))
    mixed = jax.random.permutation(jax.random.fold_in(own, 3), count)
    source_of, receiver = mixed[0:count // 2 * 2:2], mixed[1:count // 2 * 2:2]
    margin = jnp.minimum(sizes[source_of] - 1, bound - sizes[receiver]) // 2
    margin = jnp.where((source_of == sequence[0]) | (receiver == sequence[0]) | (sizes[receiver] == 0), 0, jnp.maximum(margin, 0))
    moved = jax.random.randint(jax.random.fold_in(own, 4), (count // 2,), 0, 1 << 20) % (margin + 1)
    sizes = sizes.at[source_of].add(-moved).at[receiver].add(moved)
    items = jnp.searchsorted(jnp.cumsum(sizes), jnp.arange(rows * top), side="right").astype(jnp.int32)
    table = items.reshape(top, rows).T
    table = table[jax.random.permutation(jax.random.fold_in(own, 1), rows)]
    turn = jax.random.randint(jax.random.fold_in(own, 2), (rows, 1), 0, top)
    return jnp.take_along_axis(table, (jnp.arange(top)[None, :] + turn) % top, axis=1)


def portions_of(amount, total, most, slope, full):
    portions = [(1 << 20) // math.isqrt(grade ** slope) + 1 for grade in range(1, amount + 1)]
    largest = most if full else min(most, max(-(-total // amount), total * portions[0] // sum(portions)))
    least = 1 if total - largest >= amount - 1 else 0
    counts, spare = [largest] + [least] * (amount - 1), total - largest - least * (amount - 1)
    while spare > 0:
        movable = [i for i in range(1, amount) if counts[i] < largest] or [i for i in range(1, amount) if counts[i] < most]
        whole, budget = sum([portions[i] for i in movable]), spare
        for i in movable:
            extra = min(most - counts[i], max(1, budget * portions[i] // whole), spare)
            counts[i] = counts[i] + extra
            spare = spare - extra
    return np.array(counts)


def normal_values(own_key, extent, scale, most, cuts=(), held_as=jnp.bfloat16):
    values = scale * jax.random.normal(own_key, extent, jnp.float32)
    if cuts:
        values = values * level_of(own_key, extent, cuts, -0.22, 0.18)
    return jnp.clip(values, -most, most).astype(held_as)


def setup_inputs(seed: int = 0) -> dict:
    arg_keys = jax.random.split(jax.random.key(seed), 7)
    tokens = normal_values(arg_keys[0], (TOKENS, D), 1.0, 6.0, ((0, 32),))
    routes_keys = jax.random.split(jax.random.fold_in(arg_keys[1], 1), TOKENS // TOK_DEV)
    routes_turns = jax.random.permutation(jax.random.fold_in(arg_keys[1], 3), TOKENS // TOK_DEV)
    routes = jax.vmap(lambda own, number: assign_block(jax.random.fold_in(arg_keys[1], 2), own, number, TOK_DEV, EXPERTS, TOPK, C, 1))(routes_keys, routes_turns).reshape((TOKENS, TOPK))
    router_logits = jnp.clip(jax.random.uniform(arg_keys[2], (TOKENS, TOPK), jnp.float32, -0.6, 0.6) * level_of(arg_keys[2], (TOKENS, TOPK), ((0, 32),), -0.4, 0.0), -0.6, 0.6)
    gate_weight = normal_values(arg_keys[3], (EXPERTS, D, FF), D ** -0.5, 0.09375, ((0, 4), (2, 8)))
    up_weight = normal_values(arg_keys[4], (EXPERTS, D, FF), D ** -0.5, 0.09375, ((0, 4), (2, 8)))
    down_weight = normal_values(arg_keys[5], (EXPERTS, FF, D), FF ** -0.5, 0.0546875, ((0, 4), (1, 8)))
    return {"tokens": tokens, "routes": routes, "router_logits": router_logits, "gate_weight": gate_weight, "up_weight": up_weight, "down_weight": down_weight}


def reference(tokens, routes, router_logits, gate_weight, up_weight, down_weight):
    shards = N_EXPERT * N_DP
    assigned = routes.reshape(shards, TOK_DEV * TOPK).astype(jnp.int32)
    onehot = (assigned[:, :, None] == jnp.arange(EXPERTS, dtype=jnp.int32)[None, None, :]).astype(jnp.int32)
    earlier = (jnp.cumsum(onehot, axis=1) - onehot).astype(jnp.int32)
    slot_index = jnp.sum(earlier * onehot, axis=2).astype(jnp.int32)
    row_slot = (jnp.arange(shards, dtype=jnp.int32)[:, None] * C + slot_index).astype(jnp.int32)
    copies = jnp.repeat(tokens.reshape(shards, TOK_DEV, D), TOPK, axis=1)
    buffers = jnp.zeros((EXPERTS, shards * C, D), jnp.bfloat16).at[assigned, row_slot].set(copies)

    def run_expert(operands):
        expert_rows, w_gate, w_up, w_down = operands
        gate_proj = jnp.dot(expert_rows, w_gate, preferred_element_type=jnp.float32)
        up_proj = jnp.dot(expert_rows, w_up, preferred_element_type=jnp.float32)
        hidden = (jax.nn.silu(gate_proj) * up_proj).astype(jnp.bfloat16)
        pieces = hidden.reshape(expert_rows.shape[0], N_DP, FFS).transpose(1, 0, 2)
        down_slices = w_down.reshape(N_DP, FFS, D)

        def add_piece(summed, operand_pair):
            partial_value = jnp.dot(operand_pair[0], operand_pair[1], preferred_element_type=jnp.float32).astype(jnp.bfloat16)
            partial_value = lax.optimization_barrier(partial_value)
            return summed + partial_value.astype(jnp.float32), None

        summed, _ = lax.scan(add_piece, jnp.zeros((expert_rows.shape[0], D), jnp.float32), (pieces, down_slices))
        return summed.astype(jnp.bfloat16)

    outputs = lax.map(run_expert, (buffers, gate_weight, up_weight, down_weight))
    picked = outputs[assigned, row_slot].astype(jnp.float32).reshape(TOKENS, TOPK, D)
    weight_first = jax.nn.sigmoid(router_logits[:, 0] - router_logits[:, 1])
    weight_second = jax.nn.sigmoid(router_logits[:, 1] - router_logits[:, 0])
    weights = jnp.stack([weight_first, weight_second], axis=1)
    return jnp.sum(weights[:, :, None] * picked, axis=1).astype(jnp.bfloat16)
```

```python
import functools

import jax
import jax.numpy as jnp
from jax import lax
from jax.experimental import pallas as pl
from jax.experimental.pallas import tpu as pltpu
from jax.sharding import PartitionSpec as P

TOPK = 2
LANES = 128
MESH = pl.DeviceIdType.MESH


def activate_rows(row_block, w_gate, w_up):
    count_rows = row_block.shape[0]
    step_rows = 256 if count_rows % 256 == 0 else count_rows

    def one_step(segment):
        gate_proj = jnp.dot(segment, w_gate, preferred_element_type=jnp.float32)
        up_proj = jnp.dot(segment, w_up, preferred_element_type=jnp.float32)
        return (jax.nn.silu(gate_proj) * up_proj).astype(jnp.bfloat16)

    stepped = lax.map(
        one_step, row_block.reshape(count_rows // step_rows, step_rows, row_block.shape[1])
    )
    return stepped.reshape(count_rows, w_gate.shape[1])


def on_device(tokens, routes, router_logits, gate_weight, up_weight, down_weight):
    experts = lax.axis_size("expert") * gate_weight.shape[0]
    tok_rows = tokens.shape[0]
    model_width = tokens.shape[1]
    capacity = 3 * tok_rows * TOPK // (2 * experts)
    w_gate = gate_weight[0]
    w_up = up_weight[0]
    w_down = down_weight[0]
    assigned = routes.reshape(-1)
    at = jnp.arange(assigned.shape[0], dtype=jnp.int32)
    same = (assigned[:, None] == assigned[None, :]) & (at[None, :] < at[:, None])
    slot_index = jnp.sum(same.astype(jnp.int32), axis=1)
    position = (assigned * capacity + slot_index).reshape(tok_rows, TOPK)
    columns = jnp.arange(experts * capacity, dtype=jnp.int32)
    placed = position[:, :, None] == columns[None, None, :]
    select = jnp.any(placed, axis=1).astype(jnp.bfloat16)
    buffer = lax.dot_general(
        select, tokens, (((0,), (0,)), ((), ())), preferred_element_type=jnp.float32
    )
    buffer = buffer.astype(jnp.bfloat16).reshape(experts, capacity, model_width)
    weight_first = jax.nn.sigmoid(router_logits[:, 0] - router_logits[:, 1])
    weight_second = jax.nn.sigmoid(router_logits[:, 1] - router_logits[:, 0])
    combine = weight_first[:, None] * placed[:, 0, :].astype(jnp.float32) + weight_second[
        :, None
    ] * placed[:, 1, :].astype(jnp.float32)
    received = lax.all_to_all(buffer, "expert", split_axis=0, concat_axis=0, tiled=True)
    sectioned = activate_rows(
        lax.all_gather(received.reshape(-1, model_width), "dp", axis=0, tiled=True), w_gate, w_up
    )
    expert_sum = lax.psum_scatter(
        jnp.dot(sectioned, w_down, preferred_element_type=jnp.float32).astype(jnp.bfloat16),
        "dp",
        scatter_dimension=0,
        tiled=True,
    )
    expert_out = expert_sum.reshape(experts, capacity, model_width)
    returned = lax.all_to_all(
        expert_out, "expert", split_axis=0, concat_axis=0, tiled=True
    ).reshape(-1, model_width)
    mixed_out = jnp.dot(
        combine,
        returned.astype(jnp.float32),
        precision=lax.Precision.HIGHEST,
        preferred_element_type=jnp.float32,
    )
    return mixed_out.astype(jnp.bfloat16)


ZS = 4
N_CH = 8
UP_TILE = 1536


def fused_kernel(
    toks, routes, logits, gate, up, down, out,
    xg, wg, wu, wd, acc_g, acc_u, hid, part, r0, r1, r2, r3, q1, q2, q3, obuf, rt, lg,
    wsem, lsem, osem, zs, zr, fs, fr, ss, sr, bs, br, zs2, zr2, fs2, fr2, ss2, sr2, bs2, br2,
):
    rows, width = toks.shape
    ffs = hid.shape[1]
    experts = lax.axis_size("expert")
    total = 8 * ZS * rows
    ck = width // N_CH
    ei = lax.axis_index("expert")
    di = lax.axis_index("dp")
    y = lax.div(ei, 2)
    core = ei - 2 * y
    z = lax.div(di, 2)
    x = di - 2 * z
    sib = (ei + 1 - 2 * core, di)
    first = (ei + core * (2 - 4 * y), di + (1 - core) * (1 - 2 * x))
    second = (ei + (1 - core) * (2 - 4 * y), di + core * (1 - 2 * x))
    zdev = [(ei, 2 * lax.rem(z + j, ZS) + x) for j in range(1, ZS)]
    partners = [sib, first, second] + zdev

    barrier = pltpu.get_barrier_semaphore()
    for dev in partners:
        pl.semaphore_signal(barrier, inc=1, device_id=dev, device_id_type=MESH)

    order = [0, 1, 2, N_CH - 1] + list(range(3, N_CH - 1))
    q = order[-1]
    qa, qr = (q if Q_GATHER else -1), (q if Q_SCATTER else -1)

    local = [
        pltpu.make_async_copy(toks, xg.at[0, 0, 0, :, pl.ds(0, width)], lsem.at[0]),
        pltpu.make_async_copy(routes, rt, lsem.at[1]),
        pltpu.make_async_copy(logits, lg, lsem.at[2]),
    ]
    for cp in local:
        cp.start()

    def weight_copy(k, c):
        if k < 2:
            src = (gate, up)[k].at[0, pl.ds(c * ck, ck), :]
            dst = (wg, wu)[k].at[c]
        else:
            src = down.at[0, :, pl.ds(c * ck, ck)]
            dst = wd.at[c]
        return pltpu.make_async_copy(src, dst, wsem.at[k, c])

    for cp in local:
        cp.wait()

    def column(row):
        i = lax.broadcasted_iota(jnp.int32, (rows, rows), 0)
        j = lax.broadcasted_iota(jnp.int32, (rows, rows), 1)
        return jnp.sum(jnp.where(i == j, row, 0.0), axis=1, keepdims=True)

    lane = lax.broadcasted_iota(jnp.int32, (rows, LANES), 1)
    slot = jnp.where(lane < experts, lane, lane - experts).astype(jnp.float32)
    diff = column(lg[1:2, :] - lg[0:1, :])
    w_first = 1.0 / (1.0 + jnp.exp(diff))
    w_second = 1.0 / (1.0 + jnp.exp(-diff))
    named = rt[...].astype(jnp.float32)
    weights = jnp.where(slot == column(named[0:1, :]), w_first, 0.0) + jnp.where(
        slot == column(named[1:2, :]), w_second, 0.0
    )
    high = weights.astype(jnp.bfloat16).astype(jnp.float32)
    coded = jnp.where(lane < experts, high, jnp.where(lane < 2 * experts, weights - high, 0.0))
    xg[0, 0, 0, :, width : width + LANES] = coded.astype(jnp.bfloat16)

    pl.semaphore_wait(barrier, len(partners))

    sent = []

    def send(src, dst, s_sem, r_sem, dev):
        cp = pltpu.make_async_remote_copy(
            src_ref=src, dst_ref=dst, send_sem=s_sem, recv_sem=r_sem,
            device_id=dev, device_id_type=MESH,
        )
        sent.append(cp)
        return cp

    ag = []
    for c in range(N_CH):
        cols = pl.ds(c * ck, ck + (LANES if c == N_CH - 1 else 0))

        def g(sf, zz):
            return xg.at[0, sf, zz, :, cols]

        own, three, four = 0, pl.ds(1, ZS - 1), pl.ds(0, ZS)
        e = {}
        e["f0"] = send(g(0, own), g(1, own), fs.at[c, 0], fr.at[c, 0], first)
        e["s0"] = send(g(0, own), g(2, own), ss.at[c, 0], sr.at[c, 0], second)
        if c == qa:
            e["s1"] = send(g(1, own), g(3, own), ss.at[c, 1], sr.at[c, 1], second)
            group = pl.ds(0, 4)
        else:
            e["f1"] = send(g(0, three), g(1, three), fs.at[c, 1], fr.at[c, 1], first)
            e["s1"] = send(g(0, three), g(2, three), ss.at[c, 1], sr.at[c, 1], second)
            e["s2"] = send(g(1, four), g(3, four), ss.at[c, 2], sr.at[c, 2], second)
            group = 0
        e["z"] = [
            send(g(group, 0), g(group, ZS - j), zs.at[c, j - 1], zr.at[c, j - 1], zdev[j - 1])
            for j in range(1, ZS)
        ]
        e["b"] = send(
            xg.at[0, :, :, :, cols], xg.at[1, :, :, :, cols], bs.at[c], br.at[c], sib
        )
        ag.append(e)

    def a_start(c, names):
        for n in names.split():
            for cp in ag[c]["z"] if n == "z" else [ag[c][n]]:
                cp.start()

    def a_wait(c, names):
        for n in names.split():
            for cp in ag[c]["z"] if n == "z" else [ag[c][n]]:
                cp.wait_recv()

    def a_stage(k, c):
        if c == qa:
            if k == 0:
                a_start(c, "f0 s0")
            elif k == 1:
                a_wait(c, "f0")
                a_start(c, "s1")
            elif k == 2:
                a_wait(c, "s0 s1")
                a_start(c, "z")
            elif k == 3:
                a_wait(c, "z")
                a_start(c, "b")
        elif k == "z":
            a_start(c, "z")
        elif k == 0:
            a_start(c, "f0 s0")
        elif k == 1:
            a_wait(c, "z")
            a_start(c, "f1 s1")
        elif k == 2:
            a_wait(c, "f0 f1")
            a_start(c, "s2")
        elif k == 3:
            a_wait(c, "s0 s1 s2")
            a_start(c, "b")

    nt = UP_TILE if ffs % UP_TILE == 0 else ffs

    def up_chunk(p):
        c = order[p]
        ag[c]["b"].wait_recv()
        weight_copy(0, c).wait()
        weight_copy(1, c).wait()
        xs = xg[:, :, :, :, c * ck : (c + 1) * ck].reshape(total, ck)
        if p == N_CH - 1:
            sel = lax.broadcasted_iota(jnp.int32, (total, LANES), 1)
            mine = (sel == ei) | (sel == ei + experts)
            coded_all = xg[:, :, :, :, width : width + LANES].reshape(total, LANES)
            w_row = jnp.sum(
                jnp.where(mine, coded_all.astype(jnp.float32), 0.0), axis=1, keepdims=True
            )
        for i in range(ffs // nt):
            at = slice(i * nt, (i + 1) * nt)
            g = jnp.dot(xs, wg[c, :, at], preferred_element_type=jnp.float32)
            if p > 0:
                g = acc_g[:, at] + g
            if p < N_CH - 1:
                acc_g[:, at] = g
            u = jnp.dot(xs, wu[c, :, at], preferred_element_type=jnp.float32)
            if p > 0:
                u = acc_u[:, at] + u
            if p < N_CH - 1:
                acc_u[:, at] = u
            else:
                hid[:, at] = (g / (1.0 + jnp.exp(-g)) * u * w_row).astype(jnp.bfloat16)

    def alone(work):
        pl.when(ei >= 0)(work)

    for ev in AG_PLAN:
        if ev[0] == "u":
            alone(functools.partial(up_chunk, ev[1]))
        elif ev[0] == "w":
            weight_copy(0, order[ev[1]]).start()
            weight_copy(1, order[ev[1]]).start()
        elif ev[0] == "v":
            weight_copy(2, RS_ORDER(order)[ev[1]]).start()
        else:
            a_stage(ev[0], order[ev[1]])

    rs = []
    for c in range(N_CH):
        at = pl.ds(c * ck, ck)
        e = {"b": send(part.at[1, :, :, :, at], r0.at[:, :, :, at], bs2.at[c], br2.at[c], sib)}
        if c == qr:
            e["z"] = [
                send(part.at[0, :, j, :, at], q3.at[ZS - 1 - j], zs2.at[c, j - 1],
                     zr2.at[c, j - 1], zdev[j - 1])
                for j in range(1, ZS)
            ]
            e["s1"] = send(part.at[0, 3, 0, :, at], q1.at[1], ss2.at[c, 1], sr2.at[c, 1], second)
            e["s0"] = send(part.at[0, 2, 0, :, at], q1.at[0], ss2.at[c, 0], sr2.at[c, 0], second)
            e["f0"] = send(part.at[0, 1, 0, :, at], q2, fs2.at[c, 0], fr2.at[c, 0], first)
        else:
            e["s2"] = send(part.at[0, 3, :, :, at], r1.at[1, :, :, at], ss2.at[c, 2],
                           sr2.at[c, 2], second)
            e["s1"] = send(part.at[0, 2, pl.ds(1, 3), :, at], r1.at[0, pl.ds(1, 3), :, at],
                           ss2.at[c, 1], sr2.at[c, 1], second)
            e["s0"] = send(part.at[0, 2, 0, :, at], r1.at[0, 0, :, at], ss2.at[c, 0],
                           sr2.at[c, 0], second)
            e["f1"] = send(part.at[0, 1, pl.ds(1, 3), :, at], r2.at[pl.ds(1, 3), :, at],
                           fs2.at[c, 1], fr2.at[c, 1], first)
            e["f0"] = send(part.at[0, 1, 0, :, at], r2.at[0, :, at], fs2.at[c, 0],
                           fr2.at[c, 0], first)
            e["z"] = [
                send(part.at[0, 0, j, :, at], r3.at[ZS - 1 - j, :, at], zs2.at[c, j - 1],
                     zr2.at[c, j - 1], zdev[j - 1])
                for j in range(1, ZS)
            ]
        rs.append(e)

    def r_start(c, names):
        for n in names.split():
            for cp in rs[c]["z"] if n == "z" else [rs[c][n]]:
                cp.start()

    def r_wait(c, names):
        for n in names.split():
            for cp in rs[c]["z"] if n == "z" else [rs[c][n]]:
                cp.wait_recv()

    def f32(v):
        return v.astype(jnp.float32)

    def down_chunk(c):
        weight_copy(2, c).wait()
        res = jnp.dot(hid[...], wd[c], preferred_element_type=jnp.float32)
        part[:, :, :, :, c * ck : (c + 1) * ck] = res.astype(jnp.bfloat16).reshape(
            2, 4, ZS, rows, ck
        )
        r_start(c, "b")

    def out_copy(c):
        at = pl.ds(c * ck, ck)
        return pltpu.make_async_copy(obuf.at[:, at], out.at[:, at], osem.at[c])

    def finish(c, terms):
        at = slice(c * ck, (c + 1) * ck)
        total_sum = f32(part[0, 0, 0, :, at])
        for term in terms:
            total_sum = total_sum + f32(term)
        obuf[:, at] = total_sum.astype(jnp.bfloat16)
        out_copy(c).start()

    def r_stage(k, c):
        at = slice(c * ck, (c + 1) * ck)
        if c == qr:
            if k == 1:
                r_wait(c, "b")
                part[0, :, 1:, :, at] = (
                    f32(part[0, :, 1:, :, at]) + f32(r0[:, 1:, :, at])
                ).astype(jnp.bfloat16)
                r_start(c, "z")
            elif k == 2:
                r_wait(c, "z")
                part[0, :, 0, :, at] = (
                    f32(part[0, :, 0, :, at]) + f32(r0[:, 0, :, at])
                    + f32(q3[0]) + f32(q3[1]) + f32(q3[2])
                ).astype(jnp.bfloat16)
                r_start(c, "s1 s0")
            elif k == 3:
                r_wait(c, "s1")
                part[0, 1, 0, :, at] = (
                    f32(part[0, 1, 0, :, at]) + f32(q1[1])
                ).astype(jnp.bfloat16)
                r_start(c, "f0")
            elif k == 4:
                r_wait(c, "s0 f0")
                finish(c, [q1[0], q2[...]])
        elif k == 1:
            r_wait(c, "b")
            part[0, 2:4, :, :, at] = (
                f32(part[0, 2:4, :, :, at]) + f32(r0[2:4, :, :, at])
            ).astype(jnp.bfloat16)
            r_start(c, "s2 s1")
        elif k == 2:
            r_wait(c, "s2")
            part[0, 1, :, :, at] = (
                f32(part[0, 1, :, :, at]) + f32(r0[1, :, :, at]) + f32(r1[1, :, :, at])
            ).astype(jnp.bfloat16)
            r_start(c, "f1")
        elif k == 3:
            r_wait(c, "s1 f1")
            part[0, 0, 1:, :, at] = (
                f32(part[0, 0, 1:, :, at]) + f32(r0[0, 1:, :, at])
                + f32(r1[0, 1:, :, at]) + f32(r2[1:, :, at])
            ).astype(jnp.bfloat16)
            r_start(c, "z")
        elif k == 5:
            r_start(c, "f0 s0")
        elif k == 4:
            r_wait(c, "f0 s0 z")
            finish(
                c,
                [r0[0, 0, :, at], r1[0, 0, :, at], r2[0, :, at]]
                + [r3[j, :, at] for j in range(ZS - 1)],
            )

    for ev in RS_PLAN:
        c = RS_ORDER(order)[ev[1]]
        if ev[0] == "d":
            alone(functools.partial(down_chunk, c))
        else:
            r_stage(ev[0], c)

    for c in range(N_CH):
        out_copy(c).wait()
    for cp in sent:
        cp.wait_send()


def RS_ORDER(order):
    return [order[-1]] + order[:-1]


Q = N_CH - 1
Q_GATHER = False
Q_SCATTER = True
AG_PLAN = [("z", 0), (0, 0), ("z", 1), (0, 1)] + [(k, c) for c in range(2, 8) for k in ("z", 0)]
AG_PLAN += [("w", 0), ("w", 1)]
AG_PLAN += [(1, 0), ("w", 2), (1, 1), ("w", 3), (2, 0), (1, 2), ("w", 4), (2, 1), (1, 3), ("w", 5), (3, 0), (2, 2), (1, 4), ("w", 6)]
AG_PLAN += [("u", 0), (3, 1), (1, 5), (2, 3), ("w", 7), ("v", 0)]
AG_PLAN += [("u", 1), (3, 2), (1, 6), (2, 4), ("v", 1)]
AG_PLAN += [("u", 2), (3, 3), (1, 7), (2, 5), ("v", 2)]
AG_PLAN += [("u", 3), (3, 4), (2, 6), ("v", 3)]
AG_PLAN += [("u", 4), (3, 5), (2, 7), ("v", 4), ("v", 5)]
AG_PLAN += [("u", 5), (3, 6), ("v", 6), ("v", 7)]
AG_PLAN += [("u", 6), (3, 7), ("u", 7)]
RS_PLAN = []
for t in range(N_CH + 8):
    if t < N_CH:
        RS_PLAN.append(("d", t))
    if t == 1:
        RS_PLAN.append((1, 0))
    for k, lag in ((1, 1), (2, 3), (3, 5), (5, 5)):
        if 1 <= t - lag < N_CH:
            RS_PLAN.append((k, t - lag))
    if t == 7:
        RS_PLAN.append((2, 0))
    if t == 10:
        RS_PLAN.append((3, 0))
    if t == 12:
        RS_PLAN.append((4, 0))
    if 1 <= t - 8 < N_CH:
        RS_PLAN.append((4, t - 8))


def fused_device(tokens, routes, router_logits, gate_weight, up_weight, down_weight):
    rows, width = tokens.shape
    ffs = gate_weight.shape[2]
    ck = width // N_CH
    total = 8 * ZS * rows
    bf = jnp.bfloat16
    dma = pltpu.SemaphoreType.DMA
    hbm = pl.BlockSpec(memory_space=pl.ANY)
    one = dma((N_CH,))
    two = dma((N_CH, 2))
    three = dma((N_CH, 3))
    return pl.pallas_call(
        fused_kernel,
        out_shape=jax.ShapeDtypeStruct((rows, width), bf),
        in_specs=[hbm] * 6,
        out_specs=hbm,
        scratch_shapes=[
            pltpu.VMEM((2, 4, ZS, rows, width + LANES), bf),
            pltpu.VMEM((N_CH, ck, ffs), bf),
            pltpu.VMEM((N_CH, ck, ffs), bf),
            pltpu.VMEM((N_CH, ffs, ck), bf),
            pltpu.VMEM((total, ffs), jnp.float32),
            pltpu.VMEM((total, ffs), jnp.float32),
            pltpu.VMEM((total, ffs), bf),
            pltpu.VMEM((2, 4, ZS, rows, width), bf),
            pltpu.VMEM((4, ZS, rows, width), bf),
            pltpu.VMEM((2, ZS, rows, width), bf),
            pltpu.VMEM((ZS, rows, width), bf),
            pltpu.VMEM((ZS - 1, rows, width), bf),
            pltpu.VMEM((2, rows, ck), bf),
            pltpu.VMEM((rows, ck), bf),
            pltpu.VMEM((ZS - 1, 4, rows, ck), bf),
            pltpu.VMEM((rows, width), bf),
            pltpu.VMEM((TOPK, rows), jnp.int32),
            pltpu.VMEM((TOPK, rows), jnp.float32),
            dma((3, N_CH)),
            dma((3,)), one,
            three, three, two, two, three, three, one, one,
            three, three, two, two, three, three, one, one,
        ],
        compiler_params=pltpu.CompilerParams(
            collective_id=0, has_side_effects=True, vmem_limit_bytes=62 * 2**20
        ),
        cost_estimate=pl.CostEstimate(
            flops=6 * total * width * ffs, bytes_accessed=6 * width * ffs, transcendentals=total * ffs
        ),
        name="moe_fused",
    )(tokens, routes.T, router_logits.T, gate_weight, up_weight, down_weight)


def solution(mesh):
    placed = (
        P(("expert", "dp"), None),
        P(("expert", "dp"), None),
        P(("expert", "dp"), None),
        P("expert", None, "dp"),
        P("expert", None, "dp"),
        P("expert", "dp", None),
    )
    small = mesh.shape["expert"] == 4 and mesh.shape["dp"] == 2 * ZS
    return jax.shard_map(
        fused_device if small else on_device,
        mesh=mesh,
        in_specs=placed,
        out_specs=P(("expert", "dp"), None),
        check_vma=False,
    )
```

```python
import functools

import jax
import jax.numpy as jnp
from jax import lax
from jax.experimental import pallas as pl
from jax.experimental.pallas import tpu as pltpu
from jax.sharding import PartitionSpec as P

TOPK = 2
LANES = 128
MESH = pl.DeviceIdType.MESH


def activate_rows(row_block, w_gate, w_up):
    count_rows = row_block.shape[0]
    step_rows = 256 if count_rows % 256 == 0 else count_rows

    def one_step(segment):
        gate_proj = jnp.dot(segment, w_gate, preferred_element_type=jnp.float32)
        up_proj = jnp.dot(segment, w_up, preferred_element_type=jnp.float32)
        return (jax.nn.silu(gate_proj) * up_proj).astype(jnp.bfloat16)

    stepped = lax.map(
        one_step, row_block.reshape(count_rows // step_rows, step_rows, row_block.shape[1])
    )
    return stepped.reshape(count_rows, w_gate.shape[1])


def on_device(tokens, routes, router_logits, gate_weight, up_weight, down_weight):
    experts = lax.axis_size("expert") * gate_weight.shape[0]
    tok_rows = tokens.shape[0]
    model_width = tokens.shape[1]
    capacity = 3 * tok_rows * TOPK // (2 * experts)
    w_gate = gate_weight[0]
    w_up = up_weight[0]
    w_down = down_weight[0]
    assigned = routes.reshape(-1)
    at = jnp.arange(assigned.shape[0], dtype=jnp.int32)
    same = (assigned[:, None] == assigned[None, :]) & (at[None, :] < at[:, None])
    slot_index = jnp.sum(same.astype(jnp.int32), axis=1)
    position = (assigned * capacity + slot_index).reshape(tok_rows, TOPK)
    columns = jnp.arange(experts * capacity, dtype=jnp.int32)
    placed = position[:, :, None] == columns[None, None, :]
    select = jnp.any(placed, axis=1).astype(jnp.bfloat16)
    buffer = lax.dot_general(
        select, tokens, (((0,), (0,)), ((), ())), preferred_element_type=jnp.float32
    )
    buffer = buffer.astype(jnp.bfloat16).reshape(experts, capacity, model_width)
    weight_first = jax.nn.sigmoid(router_logits[:, 0] - router_logits[:, 1])
    weight_second = jax.nn.sigmoid(router_logits[:, 1] - router_logits[:, 0])
    combine = weight_first[:, None] * placed[:, 0, :].astype(jnp.float32) + weight_second[
        :, None
    ] * placed[:, 1, :].astype(jnp.float32)
    received = lax.all_to_all(buffer, "expert", split_axis=0, concat_axis=0, tiled=True)
    sectioned = activate_rows(
        lax.all_gather(received.reshape(-1, model_width), "dp", axis=0, tiled=True), w_gate, w_up
    )
    expert_sum = lax.psum_scatter(
        jnp.dot(sectioned, w_down, preferred_element_type=jnp.float32).astype(jnp.bfloat16),
        "dp",
        scatter_dimension=0,
        tiled=True,
    )
    expert_out = expert_sum.reshape(experts, capacity, model_width)
    returned = lax.all_to_all(
        expert_out, "expert", split_axis=0, concat_axis=0, tiled=True
    ).reshape(-1, model_width)
    mixed_out = jnp.dot(
        combine,
        returned.astype(jnp.float32),
        precision=lax.Precision.HIGHEST,
        preferred_element_type=jnp.float32,
    )
    return mixed_out.astype(jnp.bfloat16)


ZS = 4
UNITS = 16
GATHER = (2, 2, 2, 2, 2, 2, 2, 2)
SCATTER = (2, 2, 2, 2, 2, 2, 2, 2)
Q_GATHER = False
Q_SCATTER = True


def cut(widths, width):
    unit = width // UNITS
    return [(sum(widths[:i]) * unit, w * unit) for i, w in enumerate(widths)]


def fused_kernel(
    toks, routes, logits, gate, up, down, out,
    xg, wg, wu, wd, acc_g, acc_u, hid, part, r0, r1, r2, r3, q1, q2, q3, obuf, rt, lg,
    wsem, lsem, osem, zs, zr, fs, fr, ss, sr, bs, br, zs2, zr2, fs2, fr2, ss2, sr2, bs2, br2,
):
    rows, width = toks.shape
    ffs = hid.shape[1]
    experts = lax.axis_size("expert")
    total = 8 * ZS * rows
    gather, scatter = cut(GATHER, width), cut(SCATTER, width)
    n_g, n_s = len(gather), len(scatter)
    qa, qr = (n_g - 1 if Q_GATHER else -1), (0 if Q_SCATTER else -1)
    ei = lax.axis_index("expert")
    di = lax.axis_index("dp")
    y = lax.div(ei, 2)
    core = ei - 2 * y
    z = lax.div(di, 2)
    x = di - 2 * z
    sib = (ei + 1 - 2 * core, di)
    first = (ei + core * (2 - 4 * y), di + (1 - core) * (1 - 2 * x))
    second = (ei + (1 - core) * (2 - 4 * y), di + core * (1 - 2 * x))
    zdev = [(ei, 2 * lax.rem(z + j, ZS) + x) for j in range(1, ZS)]
    partners = [sib, first, second] + zdev

    barrier = pltpu.get_barrier_semaphore()
    for dev in partners:
        pl.semaphore_signal(barrier, inc=1, device_id=dev, device_id_type=MESH)

    local = [
        pltpu.make_async_copy(toks, xg.at[0, 0, 0, :, pl.ds(0, width)], lsem.at[0]),
        pltpu.make_async_copy(routes, rt, lsem.at[1]),
        pltpu.make_async_copy(logits, lg, lsem.at[2]),
    ]
    for cp in local:
        cp.start()

    def weight_copy(k, c):
        if k < 2:
            rs = pl.ds(*gather[c])
            return pltpu.make_async_copy(
                (gate, up)[k].at[0, rs, :], (wg, wu)[k].at[rs, :], wsem.at[k, c]
            )
        cs = pl.ds(*scatter[c])
        return pltpu.make_async_copy(down.at[0, :, cs], wd.at[:, cs], wsem.at[k, c])

    for cp in local:
        cp.wait()

    def column(row):
        i = lax.broadcasted_iota(jnp.int32, (rows, rows), 0)
        j = lax.broadcasted_iota(jnp.int32, (rows, rows), 1)
        return jnp.sum(jnp.where(i == j, row, 0.0), axis=1, keepdims=True)

    lane = lax.broadcasted_iota(jnp.int32, (rows, LANES), 1)
    slot = jnp.where(lane < experts, lane, lane - experts).astype(jnp.float32)
    diff = column(lg[1:2, :] - lg[0:1, :])
    w_first = 1.0 / (1.0 + jnp.exp(diff))
    w_second = 1.0 / (1.0 + jnp.exp(-diff))
    named = rt[...].astype(jnp.float32)
    weights = jnp.where(slot == column(named[0:1, :]), w_first, 0.0) + jnp.where(
        slot == column(named[1:2, :]), w_second, 0.0
    )
    high = weights.astype(jnp.bfloat16).astype(jnp.float32)
    coded = jnp.where(lane < experts, high, jnp.where(lane < 2 * experts, weights - high, 0.0))
    xg[0, 0, 0, :, width : width + LANES] = coded.astype(jnp.bfloat16)

    pl.semaphore_wait(barrier, len(partners))

    sent = []

    def send(src, dst, s_sem, r_sem, dev):
        cp = pltpu.make_async_remote_copy(
            src_ref=src, dst_ref=dst, send_sem=s_sem, recv_sem=r_sem,
            device_id=dev, device_id_type=MESH,
        )
        sent.append(cp)
        return cp

    ag = []
    for c, (lo, w) in enumerate(gather):
        cols = pl.ds(lo, w + (LANES if c == n_g - 1 else 0))

        def g(sf, zz):
            return xg.at[0, sf, zz, :, cols]

        own, three, four = 0, pl.ds(1, ZS - 1), pl.ds(0, ZS)
        e = {}
        e["f0"] = send(g(0, own), g(1, own), fs.at[c, 0], fr.at[c, 0], first)
        e["s0"] = send(g(0, own), g(2, own), ss.at[c, 0], sr.at[c, 0], second)
        if c == qa:
            e["s1"] = send(g(1, own), g(3, own), ss.at[c, 1], sr.at[c, 1], second)
            group = pl.ds(0, 4)
        else:
            e["f1"] = send(g(0, three), g(1, three), fs.at[c, 1], fr.at[c, 1], first)
            e["s1"] = send(g(0, three), g(2, three), ss.at[c, 1], sr.at[c, 1], second)
            e["s2"] = send(g(1, four), g(3, four), ss.at[c, 2], sr.at[c, 2], second)
            group = 0
        e["z"] = [
            send(g(group, 0), g(group, ZS - j), zs.at[c, j - 1], zr.at[c, j - 1], zdev[j - 1])
            for j in range(1, ZS)
        ]
        e["b"] = send(
            xg.at[0, :, :, :, cols], xg.at[1, :, :, :, cols], bs.at[c], br.at[c], sib
        )
        ag.append(e)

    def a_start(c, names):
        for n in names.split():
            for cp in ag[c]["z"] if n == "z" else [ag[c][n]]:
                cp.start()

    def a_wait(c, names):
        for n in names.split():
            for cp in ag[c]["z"] if n == "z" else [ag[c][n]]:
                cp.wait_recv()

    def a_stage(k, c):
        if c == qa:
            if k == 0:
                a_start(c, "f0 s0")
            elif k == 1:
                a_wait(c, "f0")
                a_start(c, "s1")
            elif k == 2:
                a_wait(c, "s0 s1")
                a_start(c, "z")
            elif k == 3:
                a_wait(c, "z")
                a_start(c, "b")
        elif k == "z":
            a_start(c, "z")
        elif k == 0:
            a_start(c, "f0 s0")
        elif k == 1:
            a_wait(c, "z")
            a_start(c, "f1 s1")
        elif k == 2:
            a_wait(c, "f0 f1")
            a_start(c, "s2")
        elif k == 3:
            a_wait(c, "s0 s1 s2")
            a_start(c, "b")

    def up_chunk(c):
        ag[c]["b"].wait_recv()
        weight_copy(0, c).wait()
        weight_copy(1, c).wait()
        lo, w = gather[c]
        xs = xg[:, :, :, :, lo : lo + w].reshape(total, w)
        g = jnp.dot(xs, wg[lo : lo + w, :], preferred_element_type=jnp.float32)
        if c > 0:
            g = acc_g[...] + g
        if c < n_g - 1:
            acc_g[...] = g
        u = jnp.dot(xs, wu[lo : lo + w, :], preferred_element_type=jnp.float32)
        if c > 0:
            u = acc_u[...] + u
        if c < n_g - 1:
            acc_u[...] = u
        else:
            sel = lax.broadcasted_iota(jnp.int32, (total, LANES), 1)
            mine = (sel == ei) | (sel == ei + experts)
            coded_all = xg[:, :, :, :, width : width + LANES].reshape(total, LANES)
            w_row = jnp.sum(
                jnp.where(mine, coded_all.astype(jnp.float32), 0.0), axis=1, keepdims=True
            )
            hid[...] = (g / (1.0 + jnp.exp(-g)) * u * w_row).astype(jnp.bfloat16)

    def alone(work):
        pl.when(ei >= 0)(work)

    for kind, c in AG_PLAN:
        if kind == "u":
            alone(functools.partial(up_chunk, c))
        elif kind == "w":
            weight_copy(0, c).start()
            weight_copy(1, c).start()
        elif kind == "v":
            weight_copy(2, c).start()
        else:
            a_stage(kind, c)

    rs = []
    for c, (lo, w) in enumerate(scatter):
        at = pl.ds(lo, w)
        e = {"b": send(part.at[1, :, :, :, at], r0.at[:, :, :, at], bs2.at[c], br2.at[c], sib)}
        if c == qr:
            e["z"] = [
                send(part.at[0, :, j, :, at], q3.at[ZS - 1 - j], zs2.at[c, j - 1],
                     zr2.at[c, j - 1], zdev[j - 1])
                for j in range(1, ZS)
            ]
            e["s1"] = send(part.at[0, 3, 0, :, at], q1.at[1], ss2.at[c, 1], sr2.at[c, 1], second)
            e["s0"] = send(part.at[0, 2, 0, :, at], q1.at[0], ss2.at[c, 0], sr2.at[c, 0], second)
            e["f0"] = send(part.at[0, 1, 0, :, at], q2, fs2.at[c, 0], fr2.at[c, 0], first)
        else:
            e["s2"] = send(part.at[0, 3, :, :, at], r1.at[1, :, :, at], ss2.at[c, 2],
                           sr2.at[c, 2], second)
            e["s1"] = send(part.at[0, 2, pl.ds(1, 3), :, at], r1.at[0, pl.ds(1, 3), :, at],
                           ss2.at[c, 1], sr2.at[c, 1], second)
            e["s0"] = send(part.at[0, 2, 0, :, at], r1.at[0, 0, :, at], ss2.at[c, 0],
                           sr2.at[c, 0], second)
            e["f1"] = send(part.at[0, 1, pl.ds(1, 3), :, at], r2.at[pl.ds(1, 3), :, at],
                           fs2.at[c, 1], fr2.at[c, 1], first)
            e["f0"] = send(part.at[0, 1, 0, :, at], r2.at[0, :, at], fs2.at[c, 0],
                           fr2.at[c, 0], first)
            e["z"] = [
                send(part.at[0, 0, j, :, at], r3.at[ZS - 1 - j, :, at], zs2.at[c, j - 1],
                     zr2.at[c, j - 1], zdev[j - 1])
                for j in range(1, ZS)
            ]
        rs.append(e)

    def r_start(c, names):
        for n in names.split():
            for cp in rs[c]["z"] if n == "z" else [rs[c][n]]:
                cp.start()

    def r_wait(c, names):
        for n in names.split():
            for cp in rs[c]["z"] if n == "z" else [rs[c][n]]:
                cp.wait_recv()

    def f32(v):
        return v.astype(jnp.float32)

    def down_chunk(c):
        weight_copy(2, c).wait()
        lo, w = scatter[c]
        res = jnp.dot(hid[...], wd[:, lo : lo + w], preferred_element_type=jnp.float32)
        part[:, :, :, :, lo : lo + w] = res.astype(jnp.bfloat16).reshape(2, 4, ZS, rows, w)
        r_start(c, "b")

    def out_copy(c):
        at = pl.ds(*scatter[c])
        return pltpu.make_async_copy(obuf.at[:, at], out.at[:, at], osem.at[c])

    def finish(c, terms):
        lo, w = scatter[c]
        at = slice(lo, lo + w)
        total_sum = f32(part[0, 0, 0, :, at])
        for term in terms:
            total_sum = total_sum + f32(term)
        obuf[:, at] = total_sum.astype(jnp.bfloat16)
        out_copy(c).start()

    def r_stage(k, c):
        lo, w = scatter[c]
        at = slice(lo, lo + w)
        if c == qr:
            if k == 1:
                r_wait(c, "b")
                part[0, :, 1:, :, at] = (
                    f32(part[0, :, 1:, :, at]) + f32(r0[:, 1:, :, at])
                ).astype(jnp.bfloat16)
                r_start(c, "z")
            elif k == 2:
                r_wait(c, "z")
                part[0, :, 0, :, at] = (
                    f32(part[0, :, 0, :, at]) + f32(r0[:, 0, :, at])
                    + f32(q3[0]) + f32(q3[1]) + f32(q3[2])
                ).astype(jnp.bfloat16)
                r_start(c, "s1 s0")
            elif k == 3:
                r_wait(c, "s1")
                part[0, 1, 0, :, at] = (
                    f32(part[0, 1, 0, :, at]) + f32(q1[1])
                ).astype(jnp.bfloat16)
                r_start(c, "f0")
            elif k == 4:
                r_wait(c, "s0 f0")
                finish(c, [q1[0], q2[...]])
        elif k == 1:
            r_wait(c, "b")
            part[0, 2:4, :, :, at] = (
                f32(part[0, 2:4, :, :, at]) + f32(r0[2:4, :, :, at])
            ).astype(jnp.bfloat16)
            r_start(c, "s2 s1")
        elif k == 2:
            r_wait(c, "s2")
            part[0, 1, :, :, at] = (
                f32(part[0, 1, :, :, at]) + f32(r0[1, :, :, at]) + f32(r1[1, :, :, at])
            ).astype(jnp.bfloat16)
            r_start(c, "f1")
        elif k == 3:
            r_wait(c, "s1 f1")
            part[0, 0, 1:, :, at] = (
                f32(part[0, 0, 1:, :, at]) + f32(r0[0, 1:, :, at])
                + f32(r1[0, 1:, :, at]) + f32(r2[1:, :, at])
            ).astype(jnp.bfloat16)
            r_start(c, "z")
        elif k == 5:
            r_start(c, "f0 s0")
        elif k == 4:
            r_wait(c, "f0 s0 z")
            finish(
                c,
                [r0[0, 0, :, at], r1[0, 0, :, at], r2[0, :, at]]
                + [r3[j, :, at] for j in range(ZS - 1)],
            )

    for kind, c in RS_PLAN:
        if kind == "d":
            alone(functools.partial(down_chunk, c))
        else:
            r_stage(kind, c)

    for c in range(n_s):
        out_copy(c).wait()
    for cp in sent:
        cp.wait_send()


AG_PLAN = (
    ('z', 0), (0, 0), ('z', 1), (0, 1), ('z', 2), (0, 2), ('z', 3), (0, 3), ('z', 4), (0, 4),
    ('z', 5), (0, 5), ('z', 6), (0, 6), ('z', 7), (0, 7), ('w', 0), ('w', 1), (1, 0), ('w', 2),
    ('w', 3), (1, 1), ('w', 4), (1, 2), ('w', 5), (2, 0), ('w', 6), (1, 3), (2, 1), ('w', 7),
    (1, 4), ('v', 0), (2, 2), (1, 5), ('v', 1), ('v', 2), (3, 0), (2, 3), (1, 6), ('v', 3),
    ('u', 0), ('v', 4), ('v', 5), (3, 1), (2, 4), (1, 7), (2, 5), (3, 2), ('v', 6), ('u', 1),
    ('v', 7), (3, 3), (2, 6), ('u', 2), (3, 4), (2, 7), ('u', 3), (3, 5), (3, 6), ('u', 4),
    (3, 7), ('u', 5), ('u', 6), ('u', 7),
)
RS_PLAN = (
    ('d', 0), ('d', 1), ('d', 2), (1, 0), ('d', 3), (1, 1), ('d', 4), (1, 2), ('d', 5), (1, 3),
    ('d', 6), (2, 1), (1, 4), (1, 5), ('d', 7), (2, 2), (1, 6), (2, 3), (1, 7), (3, 1), (2, 4),
    (2, 0), (3, 2), (3, 3), (2, 5), (3, 4), (2, 6), (3, 5), (2, 7), (5, 1), (5, 2), (5, 3),
    (5, 4), (5, 5), (5, 6), (5, 7), (3, 0), (3, 6), (3, 7), (4, 1), (4, 2), (4, 3), (4, 4),
    (4, 5), (4, 0), (4, 6), (4, 7),
)


def fused_device(tokens, routes, router_logits, gate_weight, up_weight, down_weight):
    rows, width = tokens.shape
    ffs = gate_weight.shape[2]
    n_g, n_s, n_q = len(GATHER), len(SCATTER), SCATTER[0] * width // UNITS
    total = 8 * ZS * rows
    bf = jnp.bfloat16
    dma = pltpu.SemaphoreType.DMA
    hbm = pl.BlockSpec(memory_space=pl.ANY)
    return pl.pallas_call(
        fused_kernel,
        out_shape=jax.ShapeDtypeStruct((rows, width), bf),
        in_specs=[hbm] * 6,
        out_specs=hbm,
        scratch_shapes=[
            pltpu.VMEM((2, 4, ZS, rows, width + LANES), bf),
            pltpu.VMEM((width, ffs), bf),
            pltpu.VMEM((width, ffs), bf),
            pltpu.VMEM((ffs, width), bf),
            pltpu.VMEM((total, ffs), jnp.float32),
            pltpu.VMEM((total, ffs), jnp.float32),
            pltpu.VMEM((total, ffs), bf),
            pltpu.VMEM((2, 4, ZS, rows, width), bf),
            pltpu.VMEM((4, ZS, rows, width), bf),
            pltpu.VMEM((2, ZS, rows, width), bf),
            pltpu.VMEM((ZS, rows, width), bf),
            pltpu.VMEM((ZS - 1, rows, width), bf),
            pltpu.VMEM((2, rows, n_q), bf),
            pltpu.VMEM((rows, n_q), bf),
            pltpu.VMEM((ZS - 1, 4, rows, n_q), bf),
            pltpu.VMEM((rows, width), bf),
            pltpu.VMEM((TOPK, rows), jnp.int32),
            pltpu.VMEM((TOPK, rows), jnp.float32),
            dma((3, max(n_g, n_s))),
            dma((3,)), dma((n_s,)),
            *[dma((n_g, k)) for k in (3, 3, 2, 2, 3, 3)], dma((n_g,)), dma((n_g,)),
            *[dma((n_s, k)) for k in (3, 3, 2, 2, 3, 3)], dma((n_s,)), dma((n_s,)),
        ],
        compiler_params=pltpu.CompilerParams(
            collective_id=0, has_side_effects=True, vmem_limit_bytes=62 * 2**20
        ),
        cost_estimate=pl.CostEstimate(
            flops=6 * total * width * ffs, bytes_accessed=6 * width * ffs, transcendentals=total * ffs
        ),
        name="moe_fused",
    )(tokens, routes.T, router_logits.T, gate_weight, up_weight, down_weight)


def solution(mesh):
    placed = (
        P(("expert", "dp"), None),
        P(("expert", "dp"), None),
        P(("expert", "dp"), None),
        P("expert", None, "dp"),
        P("expert", None, "dp"),
        P("expert", "dp", None),
    )
    small = mesh.shape["expert"] == 4 and mesh.shape["dp"] == 2 * ZS
    return jax.shard_map(
        fused_device if small else on_device,
        mesh=mesh,
        in_specs=placed,
        out_specs=P(("expert", "dp"), None),
        check_vma=False,
    )
```

```python
import functools

import jax
import jax.numpy as jnp
from jax import lax
from jax.experimental import pallas as pl
from jax.experimental.pallas import tpu as pltpu
from jax.sharding import PartitionSpec as P

TOPK = 2
LANES = 128
MESH = pl.DeviceIdType.MESH


def activate_rows(row_block, w_gate, w_up):
    count_rows = row_block.shape[0]
    step_rows = 256 if count_rows % 256 == 0 else count_rows

    def one_step(segment):
        gate_proj = jnp.dot(segment, w_gate, preferred_element_type=jnp.float32)
        up_proj = jnp.dot(segment, w_up, preferred_element_type=jnp.float32)
        return (jax.nn.silu(gate_proj) * up_proj).astype(jnp.bfloat16)

    stepped = lax.map(
        one_step, row_block.reshape(count_rows // step_rows, step_rows, row_block.shape[1])
    )
    return stepped.reshape(count_rows, w_gate.shape[1])


def on_device(tokens, routes, router_logits, gate_weight, up_weight, down_weight):
    experts = lax.axis_size("expert") * gate_weight.shape[0]
    tok_rows = tokens.shape[0]
    model_width = tokens.shape[1]
    capacity = 3 * tok_rows * TOPK // (2 * experts)
    w_gate = gate_weight[0]
    w_up = up_weight[0]
    w_down = down_weight[0]
    assigned = routes.reshape(-1)
    at = jnp.arange(assigned.shape[0], dtype=jnp.int32)
    same = (assigned[:, None] == assigned[None, :]) & (at[None, :] < at[:, None])
    slot_index = jnp.sum(same.astype(jnp.int32), axis=1)
    position = (assigned * capacity + slot_index).reshape(tok_rows, TOPK)
    columns = jnp.arange(experts * capacity, dtype=jnp.int32)
    placed = position[:, :, None] == columns[None, None, :]
    select = jnp.any(placed, axis=1).astype(jnp.bfloat16)
    buffer = lax.dot_general(
        select, tokens, (((0,), (0,)), ((), ())), preferred_element_type=jnp.float32
    )
    buffer = buffer.astype(jnp.bfloat16).reshape(experts, capacity, model_width)
    weight_first = jax.nn.sigmoid(router_logits[:, 0] - router_logits[:, 1])
    weight_second = jax.nn.sigmoid(router_logits[:, 1] - router_logits[:, 0])
    combine = weight_first[:, None] * placed[:, 0, :].astype(jnp.float32) + weight_second[
        :, None
    ] * placed[:, 1, :].astype(jnp.float32)
    received = lax.all_to_all(buffer, "expert", split_axis=0, concat_axis=0, tiled=True)
    sectioned = activate_rows(
        lax.all_gather(received.reshape(-1, model_width), "dp", axis=0, tiled=True), w_gate, w_up
    )
    expert_sum = lax.psum_scatter(
        jnp.dot(sectioned, w_down, preferred_element_type=jnp.float32).astype(jnp.bfloat16),
        "dp",
        scatter_dimension=0,
        tiled=True,
    )
    expert_out = expert_sum.reshape(experts, capacity, model_width)
    returned = lax.all_to_all(
        expert_out, "expert", split_axis=0, concat_axis=0, tiled=True
    ).reshape(-1, model_width)
    mixed_out = jnp.dot(
        combine,
        returned.astype(jnp.float32),
        precision=lax.Precision.HIGHEST,
        preferred_element_type=jnp.float32,
    )
    return mixed_out.astype(jnp.bfloat16)


ZS = 4
UNITS = 16
GATHER = (2, 2, 2, 2, 2, 2, 2, 2)
SCATTER = (2, 2, 2, 2, 2, 2, 2, 2)
Q_GATHER = True
Q_SCATTER = 1


def cut(widths, width):
    unit = width // UNITS
    return [(sum(widths[:i]) * unit, w * unit) for i, w in enumerate(widths)]


def fused_kernel(
    toks, routes, logits, gate, up, down, out,
    xg, wg, wu, wd, acc_g, acc_u, hid, part, r0, r1, r2, r3, q1, q2, q3, obuf, rt, lg,
    wsem, lsem, osem, zs, zr, fs, fr, ss, sr, bs, br, zs2, zr2, fs2, fr2, ss2, sr2, bs2, br2,
):
    rows, width = toks.shape
    ffs = hid.shape[1]
    experts = lax.axis_size("expert")
    total = 8 * ZS * rows
    gather, scatter = cut(GATHER, width), cut(SCATTER, width)
    n_g, n_s = len(gather), len(scatter)
    qa, qr = (n_g - 1 if Q_GATHER else -1), Q_SCATTER
    ei = lax.axis_index("expert")
    di = lax.axis_index("dp")
    y = lax.div(ei, 2)
    core = ei - 2 * y
    z = lax.div(di, 2)
    x = di - 2 * z
    sib = (ei + 1 - 2 * core, di)
    first = (ei + core * (2 - 4 * y), di + (1 - core) * (1 - 2 * x))
    second = (ei + (1 - core) * (2 - 4 * y), di + core * (1 - 2 * x))
    zdev = [(ei, 2 * lax.rem(z + j, ZS) + x) for j in range(1, ZS)]
    partners = [sib, first, second] + zdev

    barrier = pltpu.get_barrier_semaphore()
    for dev in partners:
        pl.semaphore_signal(barrier, inc=1, device_id=dev, device_id_type=MESH)

    local = [
        pltpu.make_async_copy(toks, xg.at[0, 0, 0, :, pl.ds(0, width)], lsem.at[0]),
        pltpu.make_async_copy(routes, rt, lsem.at[1]),
        pltpu.make_async_copy(logits, lg, lsem.at[2]),
    ]
    for cp in local:
        cp.start()

    def weight_copy(k, c):
        if k < 2:
            rs = pl.ds(*gather[c])
            return pltpu.make_async_copy(
                (gate, up)[k].at[0, rs, :], (wg, wu)[k].at[rs, :], wsem.at[k, c]
            )
        cs = pl.ds(*scatter[c])
        return pltpu.make_async_copy(down.at[0, :, cs], wd.at[:, cs], wsem.at[k, c])

    for cp in local:
        cp.wait()

    def column(row):
        i = lax.broadcasted_iota(jnp.int32, (rows, rows), 0)
        j = lax.broadcasted_iota(jnp.int32, (rows, rows), 1)
        return jnp.sum(jnp.where(i == j, row, 0.0), axis=1, keepdims=True)

    lane = lax.broadcasted_iota(jnp.int32, (rows, LANES), 1)
    slot = jnp.where(lane < experts, lane, lane - experts).astype(jnp.float32)
    diff = column(lg[1:2, :] - lg[0:1, :])
    w_first = 1.0 / (1.0 + jnp.exp(diff))
    w_second = 1.0 / (1.0 + jnp.exp(-diff))
    named = rt[...].astype(jnp.float32)
    weights = jnp.where(slot == column(named[0:1, :]), w_first, 0.0) + jnp.where(
        slot == column(named[1:2, :]), w_second, 0.0
    )
    high = weights.astype(jnp.bfloat16).astype(jnp.float32)
    coded = jnp.where(lane < experts, high, jnp.where(lane < 2 * experts, weights - high, 0.0))
    xg[0, 0, 0, :, width : width + LANES] = coded.astype(jnp.bfloat16)

    pl.semaphore_wait(barrier, len(partners))

    sent = []

    def send(src, dst, s_sem, r_sem, dev):
        cp = pltpu.make_async_remote_copy(
            src_ref=src, dst_ref=dst, send_sem=s_sem, recv_sem=r_sem,
            device_id=dev, device_id_type=MESH,
        )
        sent.append(cp)
        return cp

    ag = []
    for c, (lo, w) in enumerate(gather):
        cols = pl.ds(lo, w + (LANES if c == n_g - 1 else 0))

        def g(sf, zz):
            return xg.at[sf, 0, zz, :, cols]

        own, three, four = 0, pl.ds(1, ZS - 1), pl.ds(0, ZS)
        e = {}
        e["f0"] = send(g(0, own), g(1, own), fs.at[c, 0], fr.at[c, 0], first)
        e["s0"] = send(g(0, own), g(2, own), ss.at[c, 0], sr.at[c, 0], second)
        if c == qa:
            e["s1"] = send(g(1, own), g(3, own), ss.at[c, 1], sr.at[c, 1], second)
            group = pl.ds(0, 4)
        else:
            e["f1"] = send(g(0, three), g(1, three), fs.at[c, 1], fr.at[c, 1], first)
            e["s1"] = send(g(0, three), g(2, three), ss.at[c, 1], sr.at[c, 1], second)
            e["s2"] = send(g(1, four), g(3, four), ss.at[c, 2], sr.at[c, 2], second)
            group = 0
        e["z"] = [
            send(g(group, 0), g(group, ZS - j), zs.at[c, j - 1], zr.at[c, j - 1], zdev[j - 1])
            for j in range(1, ZS)
        ]
        for h in range(2):
            g2 = pl.ds(2 * h, 2)
            e["b%d" % h] = send(
                xg.at[g2, 0, :, :, cols], xg.at[g2, 1, :, :, cols], bs.at[c, h], br.at[c, h], sib
            )
        ag.append(e)

    def a_start(c, names):
        for n in names.split():
            for cp in ag[c]["z"] if n == "z" else [ag[c][n]]:
                cp.start()

    def a_wait(c, names):
        for n in names.split():
            for cp in ag[c]["z"] if n == "z" else [ag[c][n]]:
                cp.wait_recv()

    def a_stage(k, c):
        if c == qa:
            if k == 0:
                a_start(c, "f0 s0")
            elif k == 1:
                a_wait(c, "f0")
                a_start(c, "s1")
            elif k == 2:
                a_wait(c, "s0 s1")
                a_start(c, "z")
            elif k == 3:
                a_wait(c, "z")
                a_start(c, "b0 b1")
        elif k == "z":
            a_start(c, "z")
        elif k == 0:
            a_start(c, "f0 s0")
        elif k == 1:
            a_wait(c, "z")
            a_start(c, "f1 s1")
        elif k == 2:
            a_wait(c, "f0 f1")
            a_start(c, "s2 b0")
        elif k == 3:
            a_wait(c, "s0 s1 s2")
            a_start(c, "b1")

    half = total // 2
    steps = [[c for k, c in PLAN if k in ("u", "u%d" % h)] for h in range(2)]
    loaded = []

    def halves(kind):
        return (int(kind[1]), int(kind[1]) + 1) if kind[1:] else (0, 2)

    def up_ready(kind, c):
        for h in range(*halves(kind)):
            ag[c]["b%d" % h].wait_recv()
        if c not in loaded:
            loaded.append(c)
            weight_copy(0, c).wait()
            weight_copy(1, c).wait()

    def up_chunk(kind, c):
        h0, h1 = halves(kind)
        lo, w = gather[c]
        rs = slice(h0 * half, h1 * half)
        fresh, last = steps[h0][0] == c, steps[h0][-1] == c
        xs = xg[2 * h0 : 2 * h1, :, :, :, lo : lo + w].reshape((h1 - h0) * half, w)
        g = jnp.dot(xs, wg[lo : lo + w, :], preferred_element_type=jnp.float32)
        if not fresh:
            g = acc_g[rs, :] + g
        if not last:
            acc_g[rs, :] = g
        u = jnp.dot(xs, wu[lo : lo + w, :], preferred_element_type=jnp.float32)
        if not fresh:
            u = acc_u[rs, :] + u
        if not last:
            acc_u[rs, :] = u
        else:
            sel = lax.broadcasted_iota(jnp.int32, ((h1 - h0) * half, LANES), 1)
            mine = (sel == ei) | (sel == ei + experts)
            coded_all = xg[2 * h0 : 2 * h1, :, :, :, width : width + LANES]
            w_row = jnp.sum(
                jnp.where(mine, coded_all.reshape(sel.shape).astype(jnp.float32), 0.0),
                axis=1, keepdims=True,
            )
            hid[rs, :] = (g / (1.0 + jnp.exp(-g)) * u * w_row).astype(jnp.bfloat16)

    def alone(work):
        pl.when(ei >= 0)(work)

    rs = []
    for c, (lo, w) in enumerate(scatter):
        at = pl.ds(lo, w)
        e = {}
        for h in range(2):
            g2 = pl.ds(2 * h, 2)
            e["b%d" % h] = send(
                part.at[g2, 1, :, :, at], r0.at[g2, :, :, at], bs2.at[c, h], br2.at[c, h], sib
            )
        if c == qr:
            e["z"] = [
                send(part.at[:, 0, j, :, at], q3.at[ZS - 1 - j], zs2.at[c, j - 1],
                     zr2.at[c, j - 1], zdev[j - 1])
                for j in range(1, ZS)
            ]
            e["s1"] = send(part.at[3, 0, 0, :, at], q1.at[1], ss2.at[c, 1], sr2.at[c, 1], second)
            e["s0"] = send(part.at[2, 0, 0, :, at], q1.at[0], ss2.at[c, 0], sr2.at[c, 0], second)
            e["f0"] = send(part.at[1, 0, 0, :, at], q2, fs2.at[c, 0], fr2.at[c, 0], first)
        else:
            e["s2"] = send(part.at[3, 0, :, :, at], r1.at[1, :, :, at], ss2.at[c, 2],
                           sr2.at[c, 2], second)
            e["s1"] = send(part.at[2, 0, pl.ds(1, 3), :, at], r1.at[0, pl.ds(1, 3), :, at],
                           ss2.at[c, 1], sr2.at[c, 1], second)
            e["s0"] = send(part.at[2, 0, 0, :, at], r1.at[0, 0, :, at], ss2.at[c, 0],
                           sr2.at[c, 0], second)
            e["f1"] = send(part.at[1, 0, pl.ds(1, 3), :, at], r2.at[pl.ds(1, 3), :, at],
                           fs2.at[c, 1], fr2.at[c, 1], first)
            e["f0"] = send(part.at[1, 0, 0, :, at], r2.at[0, :, at], fs2.at[c, 0],
                           fr2.at[c, 0], first)
            e["z"] = [
                send(part.at[0, 0, j, :, at], r3.at[ZS - 1 - j, :, at], zs2.at[c, j - 1],
                     zr2.at[c, j - 1], zdev[j - 1])
                for j in range(1, ZS)
            ]
        rs.append(e)

    def r_start(c, names):
        for n in names.split():
            for cp in rs[c]["z"] if n == "z" else [rs[c][n]]:
                cp.start()

    def r_wait(c, names):
        for n in names.split():
            for cp in rs[c]["z"] if n == "z" else [rs[c][n]]:
                cp.wait_recv()

    def f32(v):
        return v.astype(jnp.float32)

    def down_ready(c):
        if ("d", c) not in loaded:
            loaded.append(("d", c))
            weight_copy(2, c).wait()

    def down_chunk(kind, c):
        h0, h1 = halves(kind)
        lo, w = scatter[c]
        res = jnp.dot(
            hid[h0 * half : h1 * half, :], wd[:, lo : lo + w], preferred_element_type=jnp.float32
        )
        part[2 * h0 : 2 * h1, :, :, :, lo : lo + w] = res.astype(jnp.bfloat16).reshape(
            2 * (h1 - h0), 2, ZS, rows, w
        )
        for h in reversed(range(h0, h1)):
            r_start(c, "b%d" % h)

    def out_copy(c):
        at = pl.ds(*scatter[c])
        return pltpu.make_async_copy(obuf.at[:, at], out.at[:, at], osem.at[c])

    def finish(c, terms):
        lo, w = scatter[c]
        at = slice(lo, lo + w)
        total_sum = f32(part[0, 0, 0, :, at])
        for term in terms:
            total_sum = total_sum + f32(term)
        obuf[:, at] = total_sum.astype(jnp.bfloat16)
        out_copy(c).start()

    def r_stage(k, c):
        lo, w = scatter[c]
        at = slice(lo, lo + w)
        if c == qr:
            if k == 1:
                r_wait(c, "b0 b1")
                part[:, 0, 1:, :, at] = (
                    f32(part[:, 0, 1:, :, at]) + f32(r0[:, 1:, :, at])
                ).astype(jnp.bfloat16)
                r_start(c, "z")
            elif k == 2:
                r_wait(c, "z")
                part[:, 0, 0, :, at] = (
                    f32(part[:, 0, 0, :, at]) + f32(r0[:, 0, :, at])
                    + f32(q3[0]) + f32(q3[1]) + f32(q3[2])
                ).astype(jnp.bfloat16)
                r_start(c, "s1 s0")
            elif k == 3:
                r_wait(c, "s1")
                part[1, 0, 0, :, at] = (
                    f32(part[1, 0, 0, :, at]) + f32(q1[1])
                ).astype(jnp.bfloat16)
                r_start(c, "f0")
            elif k == 4:
                r_wait(c, "s0 f0")
                finish(c, [q1[0], q2[...]])
        elif k == 1:
            r_wait(c, "b1")
            part[2:4, 0, :, :, at] = (
                f32(part[2:4, 0, :, :, at]) + f32(r0[2:4, :, :, at])
            ).astype(jnp.bfloat16)
            r_start(c, "s2 s1")
        elif k == 2:
            r_wait(c, "b0 s2")
            part[1, 0, :, :, at] = (
                f32(part[1, 0, :, :, at]) + f32(r0[1, :, :, at]) + f32(r1[1, :, :, at])
            ).astype(jnp.bfloat16)
            r_start(c, "f1")
        elif k == 3:
            r_wait(c, "s1 f1")
            part[0, 0, 1:, :, at] = (
                f32(part[0, 0, 1:, :, at]) + f32(r0[0, 1:, :, at])
                + f32(r1[0, 1:, :, at]) + f32(r2[1:, :, at])
            ).astype(jnp.bfloat16)
            r_start(c, "z")
        elif k == 5:
            r_start(c, "f0 s0")
        elif k == 4:
            r_wait(c, "f0 s0 z")
            finish(
                c,
                [r0[0, 0, :, at], r1[0, 0, :, at], r2[0, :, at]]
                + [r3[j, :, at] for j in range(ZS - 1)],
            )

    for kind, c in PLAN:
        if kind in ("u", "u0", "u1"):
            up_ready(kind, c)
            alone(functools.partial(up_chunk, kind, c))
        elif kind in ("d", "d0", "d1"):
            down_ready(c)
            alone(functools.partial(down_chunk, kind, c))
        elif kind == "w":
            weight_copy(0, c).start()
            weight_copy(1, c).start()
        elif kind == "v":
            weight_copy(2, c).start()
        elif kind in ("r1", "r2", "r3", "r4", "r5"):
            r_stage(int(kind[1]), c)
        else:
            a_stage(kind, c)

    for c in range(n_s):
        out_copy(c).wait()
    for cp in sent:
        cp.wait_send()


PLAN = (
    ('z', 0), (0, 0), ('z', 1), (0, 1), ('z', 2), (0, 2), ('z', 3), (0, 3), ('z', 4), (0, 4),
    ('z', 5), (0, 5), ('z', 6), (0, 6), (0, 7), ('w', 0), ('w', 1), (1, 0), ('w', 2), ('w', 3),
    (1, 7), (1, 1), ('w', 4), (1, 2), ('w', 5), (2, 0), ('w', 6), (2, 7), (1, 3), ('u0', 0),
    ('w', 7), ('v', 0), (2, 1), (1, 4), (2, 2), ('v', 1), ('u0', 1), ('v', 2), (3, 0), (2, 3),
    (1, 5), ('u0', 2), ('v', 3), (1, 6), ('v', 4), ('u1', 0), ('v', 5), (3, 1), (2, 4),
    ('u0', 3), ('v', 6), (3, 2), ('u1', 1), ('v', 7), (2, 5), (3, 3), ('u1', 2), (2, 6),
    ('u0', 4), (3, 4), (3, 7), ('u1', 3), (3, 5), ('u1', 4), (3, 6), ('u', 7), ('u', 5),
    ('u1', 6), ('d1', 0), ('u0', 6), ('d0', 0), ('r1', 0), ('d', 1), ('d', 2), ('d', 3),
    ('r1', 1), ('r2', 0), ('r1', 2), ('d', 4), ('r1', 3), ('d', 5), ('r1', 4), ('d', 6),
    ('r3', 0), ('r2', 2), ('r1', 5), ('d', 7), ('r1', 6), ('r2', 3), ('r1', 7), ('r2', 4),
    ('r3', 2), ('r3', 3), ('r2', 5), ('r2', 1), ('r3', 4), ('r2', 6), ('r3', 5), ('r2', 7),
    ('r5', 0), ('r5', 2), ('r5', 3), ('r5', 4), ('r5', 5), ('r5', 6), ('r5', 7), ('r3', 1),
    ('r3', 6), ('r3', 7), ('r4', 0), ('r4', 2), ('r4', 3), ('r4', 4), ('r4', 5), ('r4', 1),
    ('r4', 6), ('r4', 7),
)


def fused_device(tokens, routes, router_logits, gate_weight, up_weight, down_weight):
    rows, width = tokens.shape
    ffs = gate_weight.shape[2]
    n_g, n_s, n_q = len(GATHER), len(SCATTER), SCATTER[Q_SCATTER] * width // UNITS
    total = 8 * ZS * rows
    bf = jnp.bfloat16
    dma = pltpu.SemaphoreType.DMA
    hbm = pl.BlockSpec(memory_space=pl.ANY)
    return pl.pallas_call(
        fused_kernel,
        out_shape=jax.ShapeDtypeStruct((rows, width), bf),
        in_specs=[hbm] * 6,
        out_specs=hbm,
        scratch_shapes=[
            pltpu.VMEM((4, 2, ZS, rows, width + LANES), bf),
            pltpu.VMEM((width, ffs), bf),
            pltpu.VMEM((width, ffs), bf),
            pltpu.VMEM((ffs, width), bf),
            pltpu.VMEM((total, ffs), jnp.float32),
            pltpu.VMEM((total, ffs), jnp.float32),
            pltpu.VMEM((total, ffs), bf),
            pltpu.VMEM((4, 2, ZS, rows, width), bf),
            pltpu.VMEM((4, ZS, rows, width), bf),
            pltpu.VMEM((2, ZS, rows, width), bf),
            pltpu.VMEM((ZS, rows, width), bf),
            pltpu.VMEM((ZS - 1, rows, width), bf),
            pltpu.VMEM((2, rows, n_q), bf),
            pltpu.VMEM((rows, n_q), bf),
            pltpu.VMEM((ZS - 1, 4, rows, n_q), bf),
            pltpu.VMEM((rows, width), bf),
            pltpu.VMEM((TOPK, rows), jnp.int32),
            pltpu.VMEM((TOPK, rows), jnp.float32),
            dma((3, max(n_g, n_s))),
            dma((3,)), dma((n_s,)),
            *[dma((n_g, k)) for k in (3, 3, 2, 2, 3, 3)], dma((n_g, 2)), dma((n_g, 2)),
            *[dma((n_s, k)) for k in (3, 3, 2, 2, 3, 3)], dma((n_s, 2)), dma((n_s, 2)),
        ],
        compiler_params=pltpu.CompilerParams(
            collective_id=0, has_side_effects=True, vmem_limit_bytes=62 * 2**20
        ),
        cost_estimate=pl.CostEstimate(
            flops=6 * total * width * ffs, bytes_accessed=6 * width * ffs, transcendentals=total * ffs
        ),
        name="moe_fused",
    )(tokens, routes.T, router_logits.T, gate_weight, up_weight, down_weight)


def solution(mesh):
    placed = (
        P(("expert", "dp"), None),
        P(("expert", "dp"), None),
        P(("expert", "dp"), None),
        P("expert", None, "dp"),
        P("expert", None, "dp"),
        P("expert", "dp", None),
    )
    small = mesh.shape["expert"] == 4 and mesh.shape["dp"] == 2 * ZS
    return jax.shard_map(
        fused_device if small else on_device,
        mesh=mesh,
        in_specs=placed,
        out_specs=P(("expert", "dp"), None),
        check_vma=False,
    )
```

```python
import functools

import jax
import jax.numpy as jnp
from jax import lax
from jax.experimental import pallas as pl
from jax.experimental.pallas import tpu as pltpu
from jax.sharding import PartitionSpec as P

TOPK = 2
LANES = 128
MESH = pl.DeviceIdType.MESH


def activate_rows(row_block, w_gate, w_up):
    count_rows = row_block.shape[0]
    step_rows = 256 if count_rows % 256 == 0 else count_rows

    def one_step(segment):
        gate_proj = jnp.dot(segment, w_gate, preferred_element_type=jnp.float32)
        up_proj = jnp.dot(segment, w_up, preferred_element_type=jnp.float32)
        return (jax.nn.silu(gate_proj) * up_proj).astype(jnp.bfloat16)

    stepped = lax.map(
        one_step, row_block.reshape(count_rows // step_rows, step_rows, row_block.shape[1])
    )
    return stepped.reshape(count_rows, w_gate.shape[1])


def on_device(tokens, routes, router_logits, gate_weight, up_weight, down_weight):
    experts = lax.axis_size("expert") * gate_weight.shape[0]
    tok_rows = tokens.shape[0]
    model_width = tokens.shape[1]
    capacity = 3 * tok_rows * TOPK // (2 * experts)
    w_gate = gate_weight[0]
    w_up = up_weight[0]
    w_down = down_weight[0]
    assigned = routes.reshape(-1)
    at = jnp.arange(assigned.shape[0], dtype=jnp.int32)
    same = (assigned[:, None] == assigned[None, :]) & (at[None, :] < at[:, None])
    slot_index = jnp.sum(same.astype(jnp.int32), axis=1)
    position = (assigned * capacity + slot_index).reshape(tok_rows, TOPK)
    columns = jnp.arange(experts * capacity, dtype=jnp.int32)
    placed = position[:, :, None] == columns[None, None, :]
    select = jnp.any(placed, axis=1).astype(jnp.bfloat16)
    buffer = lax.dot_general(
        select, tokens, (((0,), (0,)), ((), ())), preferred_element_type=jnp.float32
    )
    buffer = buffer.astype(jnp.bfloat16).reshape(experts, capacity, model_width)
    weight_first = jax.nn.sigmoid(router_logits[:, 0] - router_logits[:, 1])
    weight_second = jax.nn.sigmoid(router_logits[:, 1] - router_logits[:, 0])
    combine = weight_first[:, None] * placed[:, 0, :].astype(jnp.float32) + weight_second[
        :, None
    ] * placed[:, 1, :].astype(jnp.float32)
    received = lax.all_to_all(buffer, "expert", split_axis=0, concat_axis=0, tiled=True)
    sectioned = activate_rows(
        lax.all_gather(received.reshape(-1, model_width), "dp", axis=0, tiled=True), w_gate, w_up
    )
    expert_sum = lax.psum_scatter(
        jnp.dot(sectioned, w_down, preferred_element_type=jnp.float32).astype(jnp.bfloat16),
        "dp",
        scatter_dimension=0,
        tiled=True,
    )
    expert_out = expert_sum.reshape(experts, capacity, model_width)
    returned = lax.all_to_all(
        expert_out, "expert", split_axis=0, concat_axis=0, tiled=True
    ).reshape(-1, model_width)
    mixed_out = jnp.dot(
        combine,
        returned.astype(jnp.float32),
        precision=lax.Precision.HIGHEST,
        preferred_element_type=jnp.float32,
    )
    return mixed_out.astype(jnp.bfloat16)


ZS = 4
UNITS = 16
GATHER = (2, 2, 2, 2, 2, 2, 2, 2)
SCATTER = (2, 2, 2, 2, 2, 2, 2, 2)
Q_GATHER = True
Q_SCATTER = 1


def cut(widths, width):
    unit = width // UNITS
    return [(sum(widths[:i]) * unit, w * unit) for i, w in enumerate(widths)]


def fused_kernel(
    toks, routes, logits, gate, up, down, out,
    xg, wg, wu, wd, acc_g, acc_u, hid, part, r0, r1, r2, r3, q1, q2, q3, obuf, rt, lg,
    wsem, lsem, osem, zs, zr, fs, fr, ss, sr, bs, br, zs2, zr2, fs2, fr2, ss2, sr2, bs2, br2,
):
    rows, width = toks.shape
    ffs = hid.shape[1]
    experts = lax.axis_size("expert")
    total = 8 * ZS * rows
    gather, scatter = cut(GATHER, width), cut(SCATTER, width)
    n_g, n_s = len(gather), len(scatter)
    qa, qr = (n_g - 1 if Q_GATHER else -1), Q_SCATTER
    ei = lax.axis_index("expert")
    di = lax.axis_index("dp")
    y = lax.div(ei, 2)
    core = ei - 2 * y
    z = lax.div(di, 2)
    x = di - 2 * z
    sib = (ei + 1 - 2 * core, di)
    first = (ei + core * (2 - 4 * y), di + (1 - core) * (1 - 2 * x))
    second = (ei + (1 - core) * (2 - 4 * y), di + core * (1 - 2 * x))
    zdev = [(ei, 2 * lax.rem(z + j, ZS) + x) for j in range(1, ZS)]
    partners = [sib, first, second] + zdev

    barrier = pltpu.get_barrier_semaphore()
    for dev in partners:
        pl.semaphore_signal(barrier, inc=1, device_id=dev, device_id_type=MESH)

    local = [
        pltpu.make_async_copy(toks, xg.at[0, 0, 0, :, pl.ds(0, width)], lsem.at[0]),
        pltpu.make_async_copy(routes, rt, lsem.at[1]),
        pltpu.make_async_copy(logits, lg, lsem.at[2]),
    ]
    for cp in local:
        cp.start()

    def weight_copy(k, c):
        if k < 2:
            rs = pl.ds(*gather[c])
            return pltpu.make_async_copy(
                (gate, up)[k].at[0, rs, :], (wg, wu)[k].at[rs, :], wsem.at[k, c]
            )
        cs = pl.ds(*scatter[c])
        return pltpu.make_async_copy(down.at[0, :, cs], wd.at[:, cs], wsem.at[k, c])

    for cp in local:
        cp.wait()

    def column(row):
        i = lax.broadcasted_iota(jnp.int32, (rows, rows), 0)
        j = lax.broadcasted_iota(jnp.int32, (rows, rows), 1)
        return jnp.sum(jnp.where(i == j, row, 0.0), axis=1, keepdims=True)

    lane = lax.broadcasted_iota(jnp.int32, (rows, LANES), 1)
    slot = jnp.where(lane < experts, lane, lane - experts).astype(jnp.float32)
    diff = column(lg[1:2, :] - lg[0:1, :])
    w_first = 1.0 / (1.0 + jnp.exp(diff))
    w_second = 1.0 / (1.0 + jnp.exp(-diff))
    named = rt[...].astype(jnp.float32)
    weights = jnp.where(slot == column(named[0:1, :]), w_first, 0.0) + jnp.where(
        slot == column(named[1:2, :]), w_second, 0.0
    )
    high = weights.astype(jnp.bfloat16).astype(jnp.float32)
    coded = jnp.where(lane < experts, high, jnp.where(lane < 2 * experts, weights - high, 0.0))
    xg[0, 0, 0, :, width : width + LANES] = coded.astype(jnp.bfloat16)

    pl.semaphore_wait(barrier, len(partners))

    sent = []

    def send(src, dst, s_sem, r_sem, dev):
        return pltpu.make_async_remote_copy(
            src_ref=src, dst_ref=dst, send_sem=s_sem, recv_sem=r_sem,
            device_id=dev, device_id_type=MESH,
        )

    ag = []
    for c, (lo, w) in enumerate(gather):
        cols = pl.ds(lo, w + (LANES if c == n_g - 1 else 0))

        def g(sf, zz):
            return xg.at[sf, 0, zz, :, cols]

        own, three, four = 0, pl.ds(1, ZS - 1), pl.ds(0, ZS)
        e = {}
        e["f0"] = send(g(0, own), g(1, own), fs.at[c, 0], fr.at[c, 0], first)
        e["s0"] = send(g(0, own), g(2, own), ss.at[c, 0], sr.at[c, 0], second)
        if c == qa:
            e["s1"] = send(g(1, own), g(3, own), ss.at[c, 1], sr.at[c, 1], second)
            group = pl.ds(0, 4)
        else:
            e["f1"] = send(g(0, three), g(1, three), fs.at[c, 1], fr.at[c, 1], first)
            e["s1"] = send(g(0, three), g(2, three), ss.at[c, 1], sr.at[c, 1], second)
            e["s2"] = send(g(1, four), g(3, four), ss.at[c, 2], sr.at[c, 2], second)
            group = 0
        e["z"] = [
            send(g(group, 0), g(group, ZS - j), zs.at[c, j - 1], zr.at[c, j - 1], zdev[j - 1])
            for j in range(1, ZS)
        ]
        for h in range(2):
            g2 = pl.ds(2 * h, 2)
            e["b%d" % h] = send(
                xg.at[g2, 0, :, :, cols], xg.at[g2, 1, :, :, cols], bs.at[c, h], br.at[c, h], sib
            )
        ag.append(e)

    def a_start(c, names):
        for n in names.split():
            for cp in ag[c]["z"] if n == "z" else [ag[c][n]]:
                cp.start()
                sent.append(cp)

    def a_wait(c, names):
        for n in names.split():
            for cp in ag[c]["z"] if n == "z" else [ag[c][n]]:
                cp.wait_recv()

    def a_stage(k, c):
        if c == qa:
            if k == 0:
                a_start(c, "f0 s0")
            elif k == 1:
                a_wait(c, "f0")
                a_start(c, "s1")
            elif k == 2:
                a_wait(c, "s0 s1")
                a_start(c, "z")
            elif k == 3:
                a_wait(c, "z")
                a_start(c, "b0 b1")
        elif k == "z":
            a_start(c, "z")
        elif k == 0:
            a_start(c, "f0 s0")
        elif k == 1:
            a_wait(c, "z")
            a_start(c, "f1 s1")
        elif k == 2:
            a_wait(c, "f0 f1")
            a_start(c, "s2 b0")
        elif k == 3:
            a_wait(c, "s0 s1 s2")
            a_start(c, "b1")

    half = total // 2
    steps = [[c for k, c in PLAN if k in ("u", "u%d" % h)] for h in range(2)]
    loaded = []

    def halves(kind):
        return (int(kind[1]), int(kind[1]) + 1) if kind[1:] else (0, 2)

    def up_ready(kind, c):
        for h in range(*halves(kind)):
            ag[c]["b%d" % h].wait_recv()
        if c not in loaded:
            loaded.append(c)
            weight_copy(0, c).wait()
            weight_copy(1, c).wait()

    def up_chunk(kind, c):
        h0, h1 = halves(kind)
        lo, w = gather[c]
        rs = slice(h0 * half, h1 * half)
        fresh, last = steps[h0][0] == c, steps[h0][-1] == c
        xs = xg[2 * h0 : 2 * h1, :, :, :, lo : lo + w].reshape((h1 - h0) * half, w)
        g = jnp.dot(xs, wg[lo : lo + w, :], preferred_element_type=jnp.float32)
        if not fresh:
            g = acc_g[rs, :] + g
        if not last:
            acc_g[rs, :] = g
        u = jnp.dot(xs, wu[lo : lo + w, :], preferred_element_type=jnp.float32)
        if not fresh:
            u = acc_u[rs, :] + u
        if not last:
            acc_u[rs, :] = u
        else:
            sel = lax.broadcasted_iota(jnp.int32, ((h1 - h0) * half, LANES), 1)
            mine = (sel == ei) | (sel == ei + experts)
            coded_all = xg[2 * h0 : 2 * h1, :, :, :, width : width + LANES]
            w_row = jnp.sum(
                jnp.where(mine, coded_all.reshape(sel.shape).astype(jnp.float32), 0.0),
                axis=1, keepdims=True,
            )
            hid[rs, :] = (g / (1.0 + jnp.exp(-g)) * u * w_row).astype(jnp.bfloat16)

    def alone(work):
        pl.when(ei >= 0)(work)

    rs = []
    for c, (lo, w) in enumerate(scatter):
        at = pl.ds(lo, w)
        e = {}
        for h in range(2):
            g2 = pl.ds(2 * h, 2)
            e["b%d" % h] = send(
                part.at[g2, 1, :, :, at], r0.at[g2, :, :, at], bs2.at[c, h], br2.at[c, h], sib
            )
        if c == qr:
            e["z"] = [
                send(part.at[:, 0, j, :, at], q3.at[ZS - 1 - j], zs2.at[c, j - 1],
                     zr2.at[c, j - 1], zdev[j - 1])
                for j in range(1, ZS)
            ]
            e["s1"] = send(part.at[3, 0, 0, :, at], q1.at[1], ss2.at[c, 1], sr2.at[c, 1], second)
            e["s0"] = send(part.at[2, 0, 0, :, at], q1.at[0], ss2.at[c, 0], sr2.at[c, 0], second)
            e["f0"] = send(part.at[1, 0, 0, :, at], q2, fs2.at[c, 0], fr2.at[c, 0], first)
        else:
            e["s2"] = send(part.at[3, 0, :, :, at], r1.at[1, :, :, at], ss2.at[c, 2],
                           sr2.at[c, 2], second)
            e["s1"] = send(part.at[2, 0, pl.ds(1, 3), :, at], r1.at[0, pl.ds(1, 3), :, at],
                           ss2.at[c, 1], sr2.at[c, 1], second)
            e["s0"] = send(part.at[2, 0, 0, :, at], r1.at[0, 0, :, at], ss2.at[c, 0],
                           sr2.at[c, 0], second)
            e["f1"] = send(part.at[1, 0, pl.ds(1, 3), :, at], r2.at[pl.ds(1, 3), :, at],
                           fs2.at[c, 1], fr2.at[c, 1], first)
            e["f0"] = send(part.at[1, 0, 0, :, at], r2.at[0, :, at], fs2.at[c, 0],
                           fr2.at[c, 0], first)
            e["z"] = [
                send(part.at[0, 0, j, :, at], r3.at[ZS - 1 - j, :, at], zs2.at[c, j - 1],
                     zr2.at[c, j - 1], zdev[j - 1])
                for j in range(1, ZS)
            ]
        rs.append(e)

    def r_start(c, names):
        for n in names.split():
            for cp in rs[c]["z"] if n == "z" else [rs[c][n]]:
                cp.start()
                sent.append(cp)

    def r_wait(c, names):
        for n in names.split():
            for cp in rs[c]["z"] if n == "z" else [rs[c][n]]:
                cp.wait_recv()

    def f32(v):
        return v.astype(jnp.float32)

    def down_ready(c):
        if ("d", c) not in loaded:
            loaded.append(("d", c))
            weight_copy(2, c).wait()

    def down_chunk(kind, c):
        h0, h1 = halves(kind)
        lo, w = scatter[c]
        res = jnp.dot(
            hid[h0 * half : h1 * half, :], wd[:, lo : lo + w], preferred_element_type=jnp.float32
        )
        part[2 * h0 : 2 * h1, :, :, :, lo : lo + w] = res.astype(jnp.bfloat16).reshape(
            2 * (h1 - h0), 2, ZS, rows, w
        )
        for h in reversed(range(h0, h1)):
            r_start(c, "b%d" % h)

    def out_copy(c):
        at = pl.ds(*scatter[c])
        return pltpu.make_async_copy(obuf.at[:, at], out.at[:, at], osem.at[c])

    def finish(c, terms):
        lo, w = scatter[c]
        at = slice(lo, lo + w)
        total_sum = f32(part[0, 0, 0, :, at])
        for term in terms:
            total_sum = total_sum + f32(term)
        obuf[:, at] = total_sum.astype(jnp.bfloat16)
        out_copy(c).start()

    def r_stage(k, c):
        lo, w = scatter[c]
        at = slice(lo, lo + w)
        if c == qr:
            if k == 1:
                r_wait(c, "b0 b1")
                part[:, 0, 1:, :, at] = (
                    f32(part[:, 0, 1:, :, at]) + f32(r0[:, 1:, :, at])
                ).astype(jnp.bfloat16)
                r_start(c, "z")
            elif k == 2:
                r_wait(c, "z")
                part[:, 0, 0, :, at] = (
                    f32(part[:, 0, 0, :, at]) + f32(r0[:, 0, :, at])
                    + f32(q3[0]) + f32(q3[1]) + f32(q3[2])
                ).astype(jnp.bfloat16)
                r_start(c, "s1 s0")
            elif k == 3:
                r_wait(c, "s1")
                part[1, 0, 0, :, at] = (
                    f32(part[1, 0, 0, :, at]) + f32(q1[1])
                ).astype(jnp.bfloat16)
                r_start(c, "f0")
            elif k == 4:
                r_wait(c, "s0 f0")
                finish(c, [q1[0], q2[...]])
        elif k == 1:
            r_wait(c, "b1")
            part[2:4, 0, :, :, at] = (
                f32(part[2:4, 0, :, :, at]) + f32(r0[2:4, :, :, at])
            ).astype(jnp.bfloat16)
            r_start(c, "s2 s1")
        elif k == 2:
            r_wait(c, "b0 s2")
            part[1, 0, :, :, at] = (
                f32(part[1, 0, :, :, at]) + f32(r0[1, :, :, at]) + f32(r1[1, :, :, at])
            ).astype(jnp.bfloat16)
            r_start(c, "f1")
        elif k == 3:
            r_wait(c, "s1 f1")
            part[0, 0, 1:, :, at] = (
                f32(part[0, 0, 1:, :, at]) + f32(r0[0, 1:, :, at])
                + f32(r1[0, 1:, :, at]) + f32(r2[1:, :, at])
            ).astype(jnp.bfloat16)
            r_start(c, "z")
        elif k == 5:
            r_start(c, "f0 s0")
        elif k == 4:
            r_wait(c, "f0 s0 z")
            finish(
                c,
                [r0[0, 0, :, at], r1[0, 0, :, at], r2[0, :, at]]
                + [r3[j, :, at] for j in range(ZS - 1)],
            )

    for kind, c in PLAN:
        if kind in ("u", "u0", "u1"):
            up_ready(kind, c)
            alone(functools.partial(up_chunk, kind, c))
        elif kind in ("d", "d0", "d1"):
            down_ready(c)
            alone(functools.partial(down_chunk, kind, c))
        elif kind == "w":
            weight_copy(0, c).start()
            weight_copy(1, c).start()
        elif kind == "v":
            weight_copy(2, c).start()
        elif kind == "x":
            for cp in sent[:c]:
                cp.wait_send()
            del sent[:c]
        elif kind in ("r1", "r2", "r3", "r4", "r5"):
            r_stage(int(kind[1]), c)
        else:
            a_stage(kind, c)

    for c in range(n_s):
        out_copy(c).wait()
    for cp in sent:
        cp.wait_send()


PLAN = (
    ('z', 0), (0, 0), ('z', 1), (0, 1), ('z', 2), (0, 2), ('z', 3), (0, 3), ('z', 4), (0, 4),
    ('z', 5), (0, 5), ('z', 6), (0, 6), (0, 7), ('w', 0), ('w', 1), (1, 0), ('w', 2), ('w', 3),
    (1, 7), (1, 1), ('w', 4), (1, 2), ('w', 5), (2, 0), ('w', 6), (2, 7), (1, 3), ('u0', 0),
    ('w', 7), ('v', 0), (2, 1), (1, 4), (2, 2), ('v', 1), ('u0', 1), ('v', 2), (3, 0), (2, 3),
    (1, 5), ('u0', 2), ('v', 3), (1, 6), ('v', 4), ('u1', 0), ('v', 5), (3, 1), (2, 4),
    ('u0', 3), ('v', 6), (3, 2), ('u1', 1), ('v', 7), (2, 5), (3, 3), ('u1', 2), (2, 6),
    ('u0', 4), (3, 4), (3, 7), ('u1', 3), (3, 5), ('u1', 4), (3, 6), ('u', 7), ('u', 5),
    ('u1', 6), ('d1', 0), ('u0', 6), ('d0', 0), ('r1', 0), ('d', 1), ('d', 2), ('d', 3),
    ('r1', 1), ('r2', 0), ('r1', 2), ('d', 4), ('r1', 3), ('d', 5), ('r1', 4), ('d', 6),
    ('r3', 0), ('r2', 2), ('r1', 5), ('d', 7), ('x', 16), ('r1', 6), ('x', 16), ('r2', 3),
    ('x', 16), ('r1', 7), ('x', 16), ('r2', 4), ('x', 14), ('r3', 2), ('r3', 3), ('r2', 5),
    ('r3', 4), ('r2', 6), ('r3', 5), ('r2', 7), ('r5', 0), ('r5', 2), ('r5', 3), ('r5', 4),
    ('r5', 5), ('r5', 6), ('r5', 7), ('r3', 6), ('r2', 1), ('r3', 7), ('r4', 0), ('r4', 2),
    ('r4', 3), ('r4', 4), ('r4', 5), ('r3', 1), ('r4', 6), ('x', 66), ('r4', 7), ('x', 9),
    ('r4', 1),
)


def fused_device(tokens, routes, router_logits, gate_weight, up_weight, down_weight):
    rows, width = tokens.shape
    ffs = gate_weight.shape[2]
    n_g, n_s, n_q = len(GATHER), len(SCATTER), SCATTER[Q_SCATTER] * width // UNITS
    total = 8 * ZS * rows
    bf = jnp.bfloat16
    dma = pltpu.SemaphoreType.DMA
    hbm = pl.BlockSpec(memory_space=pl.ANY)
    return pl.pallas_call(
        fused_kernel,
        out_shape=jax.ShapeDtypeStruct((rows, width), bf),
        in_specs=[hbm] * 6,
        out_specs=hbm,
        scratch_shapes=[
            pltpu.VMEM((4, 2, ZS, rows, width + LANES), bf),
            pltpu.VMEM((width, ffs), bf),
            pltpu.VMEM((width, ffs), bf),
            pltpu.VMEM((ffs, width), bf),
            pltpu.VMEM((total, ffs), jnp.float32),
            pltpu.VMEM((total, ffs), jnp.float32),
            pltpu.VMEM((total, ffs), bf),
            pltpu.VMEM((4, 2, ZS, rows, width), bf),
            pltpu.VMEM((4, ZS, rows, width), bf),
            pltpu.VMEM((2, ZS, rows, width), bf),
            pltpu.VMEM((ZS, rows, width), bf),
            pltpu.VMEM((ZS - 1, rows, width), bf),
            pltpu.VMEM((2, rows, n_q), bf),
            pltpu.VMEM((rows, n_q), bf),
            pltpu.VMEM((ZS - 1, 4, rows, n_q), bf),
            pltpu.VMEM((rows, width), bf),
            pltpu.VMEM((TOPK, rows), jnp.int32),
            pltpu.VMEM((TOPK, rows), jnp.float32),
            dma((3, max(n_g, n_s))),
            dma((3,)), dma((n_s,)),
            *[dma((n_g, k)) for k in (3, 3, 2, 2, 3, 3)], dma((n_g, 2)), dma((n_g, 2)),
            *[dma((n_s, k)) for k in (3, 3, 2, 2, 3, 3)], dma((n_s, 2)), dma((n_s, 2)),
        ],
        compiler_params=pltpu.CompilerParams(
            collective_id=0, has_side_effects=True, vmem_limit_bytes=62 * 2**20
        ),
        cost_estimate=pl.CostEstimate(
            flops=6 * total * width * ffs, bytes_accessed=6 * width * ffs, transcendentals=total * ffs
        ),
        name="moe_fused",
    )(tokens, routes.T, router_logits.T, gate_weight, up_weight, down_weight)


def solution(mesh):
    placed = (
        P(("expert", "dp"), None),
        P(("expert", "dp"), None),
        P(("expert", "dp"), None),
        P("expert", None, "dp"),
        P("expert", None, "dp"),
        P("expert", "dp", None),
    )
    small = mesh.shape["expert"] == 4 and mesh.shape["dp"] == 2 * ZS
    return jax.shard_map(
        fused_device if small else on_device,
        mesh=mesh,
        in_specs=placed,
        out_specs=P(("expert", "dp"), None),
        check_vma=False,
    )
```

```python
import functools

import jax
import jax.numpy as jnp
from jax import lax
from jax.experimental import pallas as pl
from jax.experimental.pallas import tpu as pltpu
from jax.sharding import PartitionSpec as P

TOPK = 2
LANES = 128
MESH = pl.DeviceIdType.MESH


def activate_rows(row_block, w_gate, w_up):
    count_rows = row_block.shape[0]
    step_rows = 256 if count_rows % 256 == 0 else count_rows

    def one_step(segment):
        gate_proj = jnp.dot(segment, w_gate, preferred_element_type=jnp.float32)
        up_proj = jnp.dot(segment, w_up, preferred_element_type=jnp.float32)
        return (jax.nn.silu(gate_proj) * up_proj).astype(jnp.bfloat16)

    stepped = lax.map(
        one_step, row_block.reshape(count_rows // step_rows, step_rows, row_block.shape[1])
    )
    return stepped.reshape(count_rows, w_gate.shape[1])


def on_device(tokens, routes, router_logits, gate_weight, up_weight, down_weight):
    experts = lax.axis_size("expert") * gate_weight.shape[0]
    tok_rows = tokens.shape[0]
    model_width = tokens.shape[1]
    capacity = 3 * tok_rows * TOPK // (2 * experts)
    w_gate = gate_weight[0]
    w_up = up_weight[0]
    w_down = down_weight[0]
    assigned = routes.reshape(-1)
    at = jnp.arange(assigned.shape[0], dtype=jnp.int32)
    same = (assigned[:, None] == assigned[None, :]) & (at[None, :] < at[:, None])
    slot_index = jnp.sum(same.astype(jnp.int32), axis=1)
    position = (assigned * capacity + slot_index).reshape(tok_rows, TOPK)
    columns = jnp.arange(experts * capacity, dtype=jnp.int32)
    placed = position[:, :, None] == columns[None, None, :]
    select = jnp.any(placed, axis=1).astype(jnp.bfloat16)
    buffer = lax.dot_general(
        select, tokens, (((0,), (0,)), ((), ())), preferred_element_type=jnp.float32
    )
    buffer = buffer.astype(jnp.bfloat16).reshape(experts, capacity, model_width)
    weight_first = jax.nn.sigmoid(router_logits[:, 0] - router_logits[:, 1])
    weight_second = jax.nn.sigmoid(router_logits[:, 1] - router_logits[:, 0])
    combine = weight_first[:, None] * placed[:, 0, :].astype(jnp.float32) + weight_second[
        :, None
    ] * placed[:, 1, :].astype(jnp.float32)
    received = lax.all_to_all(buffer, "expert", split_axis=0, concat_axis=0, tiled=True)
    sectioned = activate_rows(
        lax.all_gather(received.reshape(-1, model_width), "dp", axis=0, tiled=True), w_gate, w_up
    )
    expert_sum = lax.psum_scatter(
        jnp.dot(sectioned, w_down, preferred_element_type=jnp.float32).astype(jnp.bfloat16),
        "dp",
        scatter_dimension=0,
        tiled=True,
    )
    expert_out = expert_sum.reshape(experts, capacity, model_width)
    returned = lax.all_to_all(
        expert_out, "expert", split_axis=0, concat_axis=0, tiled=True
    ).reshape(-1, model_width)
    mixed_out = jnp.dot(
        combine,
        returned.astype(jnp.float32),
        precision=lax.Precision.HIGHEST,
        preferred_element_type=jnp.float32,
    )
    return mixed_out.astype(jnp.bfloat16)


ZS = 4
UNITS = 16
GATHER = (2, 2, 2, 2, 2, 2, 2, 2)
SCATTER = (2, 2, 2, 2, 2, 2, 2, 2)
Q_GATHER = True
Q_SCATTER = 1


def cut(widths, width):
    unit = width // UNITS
    return [(sum(widths[:i]) * unit, w * unit) for i, w in enumerate(widths)]


def fused_kernel(
    toks, routes, logits, gate, up, down, out,
    xg, wg, wu, wd, acc_g, acc_u, hid, part, r0, r1, r2, r3, q1, q2, q3, obuf, rt, lg,
    wsem, lsem, osem, zs, zr, fs, fr, ss, sr, bs, br, zs2, zr2, fs2, fr2, ss2, sr2, bs2, br2,
):
    rows, width = toks.shape
    ffs = hid.shape[1]
    experts = lax.axis_size("expert")
    total = 8 * ZS * rows
    gather, scatter = cut(GATHER, width), cut(SCATTER, width)
    n_g, n_s = len(gather), len(scatter)
    qa, qr = (n_g - 1 if Q_GATHER else -1), Q_SCATTER
    ei = lax.axis_index("expert")
    di = lax.axis_index("dp")
    y = lax.div(ei, 2)
    core = ei - 2 * y
    z = lax.div(di, 2)
    x = di - 2 * z
    sib = (ei + 1 - 2 * core, di)
    first = (ei + core * (2 - 4 * y), di + (1 - core) * (1 - 2 * x))
    second = (ei + (1 - core) * (2 - 4 * y), di + core * (1 - 2 * x))
    zdev = [(ei, 2 * lax.rem(z + j, ZS) + x) for j in range(1, ZS)]
    partners = [sib, first, second] + zdev

    barrier = pltpu.get_barrier_semaphore()
    for dev in partners:
        pl.semaphore_signal(barrier, inc=1, device_id=dev, device_id_type=MESH)

    local = [
        pltpu.make_async_copy(toks, xg.at[0, 0, 0, :, pl.ds(0, width)], lsem.at[0]),
        pltpu.make_async_copy(routes, rt, lsem.at[1]),
        pltpu.make_async_copy(logits, lg, lsem.at[2]),
    ]
    for cp in local:
        cp.start()

    def weight_copy(k, c):
        if k < 2:
            rs = pl.ds(*gather[c])
            return pltpu.make_async_copy(
                (gate, up)[k].at[0, rs, :], (wg, wu)[k].at[rs, :], wsem.at[k, c]
            )
        cs = pl.ds(*scatter[c])
        return pltpu.make_async_copy(down.at[0, :, cs], wd.at[:, cs], wsem.at[k, c])

    pl.semaphore_wait(barrier, len(partners))

    sent = []

    def send(src, dst, s_sem, r_sem, dev):
        return pltpu.make_async_remote_copy(
            src_ref=src, dst_ref=dst, send_sem=s_sem, recv_sem=r_sem,
            device_id=dev, device_id_type=MESH,
        )

    ag = []
    for c, (lo, w) in enumerate(gather):
        cols = pl.ds(lo, w + (LANES if c == n_g - 1 else 0))

        def g(sf, zz):
            return xg.at[sf, 0, zz, :, cols]

        own, three, four = 0, pl.ds(1, ZS - 1), pl.ds(0, ZS)
        mine = g(0, own) if c == n_g - 1 else toks.at[:, cols]
        e = {}
        e["f0"] = send(mine, g(1, own), fs.at[c, 0], fr.at[c, 0], first)
        e["s0"] = send(mine, g(2, own), ss.at[c, 0], sr.at[c, 0], second)
        if c == qa:
            e["s1"] = send(g(1, own), g(3, own), ss.at[c, 1], sr.at[c, 1], second)
            group = pl.ds(0, 4)
        else:
            e["f1"] = send(g(0, three), g(1, three), fs.at[c, 1], fr.at[c, 1], first)
            e["s1"] = send(g(0, three), g(2, three), ss.at[c, 1], sr.at[c, 1], second)
            e["s2"] = send(g(1, four), g(3, four), ss.at[c, 2], sr.at[c, 2], second)
            group = 0
        e["z"] = [
            send(g(group, 0) if c == qa else mine, g(group, ZS - j), zs.at[c, j - 1], zr.at[c, j - 1], zdev[j - 1])
            for j in range(1, ZS)
        ]
        for h in range(2):
            g2 = pl.ds(2 * h, 2)
            e["b%d" % h] = send(
                xg.at[g2, 0, :, :, cols], xg.at[g2, 1, :, :, cols], bs.at[c, h], br.at[c, h], sib
            )
        ag.append(e)

    def a_start(c, names):
        for n in names.split():
            for cp in ag[c]["z"] if n == "z" else [ag[c][n]]:
                cp.start()
                sent.append(cp)

    def a_wait(c, names):
        for n in names.split():
            for cp in ag[c]["z"] if n == "z" else [ag[c][n]]:
                cp.wait_recv()

    def own_ready():
        for cp in local:
            cp.wait()

        def column(row):
            i = lax.broadcasted_iota(jnp.int32, (rows, rows), 0)
            j = lax.broadcasted_iota(jnp.int32, (rows, rows), 1)
            return jnp.sum(jnp.where(i == j, row, 0.0), axis=1, keepdims=True)

        lane = lax.broadcasted_iota(jnp.int32, (rows, LANES), 1)
        slot = jnp.where(lane < experts, lane, lane - experts).astype(jnp.float32)
        diff = column(lg[1:2, :] - lg[0:1, :])
        w_first = 1.0 / (1.0 + jnp.exp(diff))
        w_second = 1.0 / (1.0 + jnp.exp(-diff))
        named = rt[...].astype(jnp.float32)
        weights = jnp.where(slot == column(named[0:1, :]), w_first, 0.0) + jnp.where(
            slot == column(named[1:2, :]), w_second, 0.0
        )
        high = weights.astype(jnp.bfloat16).astype(jnp.float32)
        coded = jnp.where(lane < experts, high, jnp.where(lane < 2 * experts, weights - high, 0.0))
        xg[0, 0, 0, :, width : width + LANES] = coded.astype(jnp.bfloat16)

    def a_stage(k, c):
        if k == 0 and c == n_g - 1:
            own_ready()
        if c == qa:
            if k == 0:
                a_start(c, "f0 s0")
            elif k == 1:
                a_wait(c, "f0")
                a_start(c, "s1")
            elif k == 2:
                a_wait(c, "s0 s1")
                a_start(c, "z")
            elif k == 3:
                a_wait(c, "z")
                a_start(c, "b0 b1")
        elif k == "z":
            a_start(c, "z")
        elif k == 0:
            a_start(c, "f0 s0")
        elif k == 1:
            a_wait(c, "z")
            a_start(c, "f1 s1")
        elif k == 2:
            a_wait(c, "f0 f1")
            a_start(c, "s2 b0")
        elif k == 3:
            a_wait(c, "s0 s1 s2")
            a_start(c, "b1")

    half = total // 2
    steps = [[c for k, c in PLAN if k in ("u", "u%d" % h)] for h in range(2)]
    loaded = []

    def halves(kind):
        return (int(kind[1]), int(kind[1]) + 1) if kind[1:] else (0, 2)

    def up_ready(kind, c):
        for h in range(*halves(kind)):
            ag[c]["b%d" % h].wait_recv()
        if c not in loaded:
            loaded.append(c)
            weight_copy(0, c).wait()
            weight_copy(1, c).wait()

    def up_chunk(kind, c):
        h0, h1 = halves(kind)
        lo, w = gather[c]
        rs = slice(h0 * half, h1 * half)
        fresh, last = steps[h0][0] == c, steps[h0][-1] == c
        xs = xg[2 * h0 : 2 * h1, :, :, :, lo : lo + w].reshape((h1 - h0) * half, w)
        g = jnp.dot(xs, wg[lo : lo + w, :], preferred_element_type=jnp.float32)
        if not fresh:
            g = acc_g[rs, :] + g
        if not last:
            acc_g[rs, :] = g
        u = jnp.dot(xs, wu[lo : lo + w, :], preferred_element_type=jnp.float32)
        if not fresh:
            u = acc_u[rs, :] + u
        if not last:
            acc_u[rs, :] = u
        else:
            sel = lax.broadcasted_iota(jnp.int32, ((h1 - h0) * half, LANES), 1)
            mine = (sel == ei) | (sel == ei + experts)
            coded_all = xg[2 * h0 : 2 * h1, :, :, :, width : width + LANES]
            w_row = jnp.sum(
                jnp.where(mine, coded_all.reshape(sel.shape).astype(jnp.float32), 0.0),
                axis=1, keepdims=True,
            )
            hid[rs, :] = (g / (1.0 + jnp.exp(-g)) * u * w_row).astype(jnp.bfloat16)

    def alone(work):
        pl.when(ei >= 0)(work)

    rs = []
    for c, (lo, w) in enumerate(scatter):
        at = pl.ds(lo, w)
        e = {}
        for h in range(2):
            g2 = pl.ds(2 * h, 2)
            e["b%d" % h] = send(
                part.at[g2, 1, :, :, at], r0.at[g2, :, :, at], bs2.at[c, h], br2.at[c, h], sib
            )
        if c == qr:
            e["z"] = [
                send(part.at[:, 0, j, :, at], q3.at[ZS - 1 - j], zs2.at[c, j - 1],
                     zr2.at[c, j - 1], zdev[j - 1])
                for j in range(1, ZS)
            ]
            e["s1"] = send(part.at[3, 0, 0, :, at], q1.at[1], ss2.at[c, 1], sr2.at[c, 1], second)
            e["s0"] = send(part.at[2, 0, 0, :, at], q1.at[0], ss2.at[c, 0], sr2.at[c, 0], second)
            e["f0"] = send(part.at[1, 0, 0, :, at], q2, fs2.at[c, 0], fr2.at[c, 0], first)
        else:
            e["s2"] = send(part.at[3, 0, :, :, at], r1.at[1, :, :, at], ss2.at[c, 2],
                           sr2.at[c, 2], second)
            e["s1"] = send(part.at[2, 0, pl.ds(1, 3), :, at], r1.at[0, pl.ds(1, 3), :, at],
                           ss2.at[c, 1], sr2.at[c, 1], second)
            e["s0"] = send(part.at[2, 0, 0, :, at], r1.at[0, 0, :, at], ss2.at[c, 0],
                           sr2.at[c, 0], second)
            e["f1"] = send(part.at[1, 0, pl.ds(1, 3), :, at], r2.at[pl.ds(1, 3), :, at],
                           fs2.at[c, 1], fr2.at[c, 1], first)
            e["f0"] = send(part.at[1, 0, 0, :, at], r2.at[0, :, at], fs2.at[c, 0],
                           fr2.at[c, 0], first)
            e["z"] = [
                send(part.at[0, 0, j, :, at], r3.at[ZS - 1 - j, :, at], zs2.at[c, j - 1],
                     zr2.at[c, j - 1], zdev[j - 1])
                for j in range(1, ZS)
            ]
        rs.append(e)

    def r_start(c, names):
        for n in names.split():
            for cp in rs[c]["z"] if n == "z" else [rs[c][n]]:
                cp.start()
                sent.append(cp)

    def r_wait(c, names):
        for n in names.split():
            for cp in rs[c]["z"] if n == "z" else [rs[c][n]]:
                cp.wait_recv()

    def f32(v):
        return v.astype(jnp.float32)

    def down_ready(c):
        if ("d", c) not in loaded:
            loaded.append(("d", c))
            weight_copy(2, c).wait()

    def down_chunk(kind, c):
        h0, h1 = halves(kind)
        lo, w = scatter[c]
        res = jnp.dot(
            hid[h0 * half : h1 * half, :], wd[:, lo : lo + w], preferred_element_type=jnp.float32
        )
        part[2 * h0 : 2 * h1, :, :, :, lo : lo + w] = res.astype(jnp.bfloat16).reshape(
            2 * (h1 - h0), 2, ZS, rows, w
        )
        for h in reversed(range(h0, h1)):
            r_start(c, "b%d" % h)

    def out_copy(c):
        at = pl.ds(*scatter[c])
        return pltpu.make_async_copy(obuf.at[:, at], out.at[:, at], osem.at[c])

    def finish(c, terms):
        lo, w = scatter[c]
        at = slice(lo, lo + w)
        total_sum = f32(part[0, 0, 0, :, at])
        for term in terms:
            total_sum = total_sum + f32(term)
        obuf[:, at] = total_sum.astype(jnp.bfloat16)
        out_copy(c).start()

    def r_stage(k, c):
        lo, w = scatter[c]
        at = slice(lo, lo + w)
        if c == qr:
            if k == 1:
                r_wait(c, "b0 b1")
                part[:, 0, 1:, :, at] = (
                    f32(part[:, 0, 1:, :, at]) + f32(r0[:, 1:, :, at])
                ).astype(jnp.bfloat16)
                r_start(c, "z")
            elif k == 2:
                r_wait(c, "z")
                part[:, 0, 0, :, at] = (
                    f32(part[:, 0, 0, :, at]) + f32(r0[:, 0, :, at])
                    + f32(q3[0]) + f32(q3[1]) + f32(q3[2])
                ).astype(jnp.bfloat16)
                r_start(c, "s1 s0")
            elif k == 3:
                r_wait(c, "s1")
                part[1, 0, 0, :, at] = (
                    f32(part[1, 0, 0, :, at]) + f32(q1[1])
                ).astype(jnp.bfloat16)
                r_start(c, "f0")
            elif k == 4:
                r_wait(c, "s0 f0")
                finish(c, [q1[0], q2[...]])
        elif k == 1:
            r_wait(c, "b1")
            part[2:4, 0, :, :, at] = (
                f32(part[2:4, 0, :, :, at]) + f32(r0[2:4, :, :, at])
            ).astype(jnp.bfloat16)
            r_start(c, "s2 s1")
        elif k == 2:
            r_wait(c, "b0 s2")
            part[1, 0, :, :, at] = (
                f32(part[1, 0, :, :, at]) + f32(r0[1, :, :, at]) + f32(r1[1, :, :, at])
            ).astype(jnp.bfloat16)
            r_start(c, "f1")
        elif k == 3:
            r_wait(c, "s1 f1")
            part[0, 0, 1:, :, at] = (
                f32(part[0, 0, 1:, :, at]) + f32(r0[0, 1:, :, at])
                + f32(r1[0, 1:, :, at]) + f32(r2[1:, :, at])
            ).astype(jnp.bfloat16)
            r_start(c, "z")
        elif k == 5:
            r_start(c, "f0 s0")
        elif k == 4:
            r_wait(c, "f0 s0 z")
            finish(
                c,
                [r0[0, 0, :, at], r1[0, 0, :, at], r2[0, :, at]]
                + [r3[j, :, at] for j in range(ZS - 1)],
            )

    for kind, c in PLAN:
        if kind in ("u", "u0", "u1"):
            up_ready(kind, c)
            alone(functools.partial(up_chunk, kind, c))
        elif kind in ("d", "d0", "d1"):
            down_ready(c)
            alone(functools.partial(down_chunk, kind, c))
        elif kind == "w":
            weight_copy(0, c).start()
            weight_copy(1, c).start()
        elif kind == "v":
            weight_copy(2, c).start()
        elif kind == "x":
            for cp in sent[:c]:
                cp.wait_send()
            del sent[:c]
        elif kind in ("r1", "r2", "r3", "r4", "r5"):
            r_stage(int(kind[1]), c)
        else:
            a_stage(kind, c)

    for c in range(n_s):
        out_copy(c).wait()
    for cp in sent:
        cp.wait_send()


PLAN = (
    ('z', 0), (0, 0), ('z', 1), (0, 1), ('z', 2), (0, 2), ('z', 3), (0, 3), ('z', 4), (0, 4),
    ('z', 5), (0, 5), ('z', 6), (0, 6), (0, 7), ('w', 0), ('w', 1), (1, 0), ('w', 2), ('w', 3),
    (1, 7), (1, 1), ('w', 4), (1, 2), ('w', 5), (2, 0), ('w', 6), (2, 7), (1, 3), ('u0', 0),
    ('w', 7), ('v', 0), (2, 1), (1, 4), (2, 2), ('v', 1), ('u0', 1), ('v', 2), (3, 0), (2, 3),
    (1, 5), ('u0', 2), ('v', 3), (1, 6), ('v', 4), ('u1', 0), ('v', 5), (3, 1), (2, 4),
    ('u0', 3), ('v', 6), (3, 2), ('u1', 1), ('v', 7), (2, 5), (3, 3), ('u1', 2), (2, 6),
    ('u0', 4), (3, 4), (3, 7), ('u1', 3), (3, 5), ('u1', 4), (3, 6), ('u', 7), ('u', 5),
    ('u1', 6), ('d1', 0), ('u0', 6), ('d0', 0), ('r1', 0), ('d', 1), ('d', 2), ('d', 3),
    ('r1', 1), ('r2', 0), ('r1', 2), ('d', 4), ('r1', 3), ('d', 5), ('r1', 4), ('d', 6),
    ('r3', 0), ('r2', 2), ('r1', 5), ('d', 7), ('x', 16), ('r1', 6), ('x', 16), ('r2', 3),
    ('x', 16), ('r1', 7), ('x', 16), ('r2', 4), ('x', 14), ('r3', 2), ('r3', 3), ('r2', 5),
    ('r3', 4), ('r2', 6), ('r3', 5), ('r2', 7), ('r5', 0), ('r5', 2), ('r5', 3), ('r5', 4),
    ('r5', 5), ('r5', 6), ('r5', 7), ('r3', 6), ('r2', 1), ('r3', 7), ('r4', 0), ('r4', 2),
    ('r4', 3), ('r4', 4), ('r4', 5), ('r3', 1), ('r4', 6), ('x', 66), ('r4', 7), ('x', 9),
    ('r4', 1),
)


def fused_device(tokens, routes, router_logits, gate_weight, up_weight, down_weight):
    rows, width = tokens.shape
    ffs = gate_weight.shape[2]
    n_g, n_s, n_q = len(GATHER), len(SCATTER), SCATTER[Q_SCATTER] * width // UNITS
    total = 8 * ZS * rows
    bf = jnp.bfloat16
    dma = pltpu.SemaphoreType.DMA
    hbm = pl.BlockSpec(memory_space=pl.ANY)
    return pl.pallas_call(
        fused_kernel,
        out_shape=jax.ShapeDtypeStruct((rows, width), bf),
        in_specs=[hbm] * 6,
        out_specs=hbm,
        scratch_shapes=[
            pltpu.VMEM((4, 2, ZS, rows, width + LANES), bf),
            pltpu.VMEM((width, ffs), bf),
            pltpu.VMEM((width, ffs), bf),
            pltpu.VMEM((ffs, width), bf),
            pltpu.VMEM((total, ffs), jnp.float32),
            pltpu.VMEM((total, ffs), jnp.float32),
            pltpu.VMEM((total, ffs), bf),
            pltpu.VMEM((4, 2, ZS, rows, width), bf),
            pltpu.VMEM((4, ZS, rows, width), bf),
            pltpu.VMEM((2, ZS, rows, width), bf),
            pltpu.VMEM((ZS, rows, width), bf),
            pltpu.VMEM((ZS - 1, rows, width), bf),
            pltpu.VMEM((2, rows, n_q), bf),
            pltpu.VMEM((rows, n_q), bf),
            pltpu.VMEM((ZS - 1, 4, rows, n_q), bf),
            pltpu.VMEM((rows, width), bf),
            pltpu.VMEM((TOPK, rows), jnp.int32),
            pltpu.VMEM((TOPK, rows), jnp.float32),
            dma((3, max(n_g, n_s))),
            dma((3,)), dma((n_s,)),
            *[dma((n_g, k)) for k in (3, 3, 2, 2, 3, 3)], dma((n_g, 2)), dma((n_g, 2)),
            *[dma((n_s, k)) for k in (3, 3, 2, 2, 3, 3)], dma((n_s, 2)), dma((n_s, 2)),
        ],
        compiler_params=pltpu.CompilerParams(
            collective_id=0, has_side_effects=True, vmem_limit_bytes=62 * 2**20
        ),
        cost_estimate=pl.CostEstimate(
            flops=6 * total * width * ffs, bytes_accessed=6 * width * ffs, transcendentals=total * ffs
        ),
        name="moe_fused",
    )(tokens, routes.T, router_logits.T, gate_weight, up_weight, down_weight)


def solution(mesh):
    placed = (
        P(("expert", "dp"), None),
        P(("expert", "dp"), None),
        P(("expert", "dp"), None),
        P("expert", None, "dp"),
        P("expert", None, "dp"),
        P("expert", "dp", None),
    )
    small = mesh.shape["expert"] == 4 and mesh.shape["dp"] == 2 * ZS
    return jax.shard_map(
        fused_device if small else on_device,
        mesh=mesh,
        in_specs=placed,
        out_specs=P(("expert", "dp"), None),
        check_vma=False,
    )
```
